32 devices in a mesh: dp: 4 (over z), seq: 4 (over x, core), mp: 2 (over y).
Axes of the slice: x: 2, y: 2, z: 4, core: 2. Of those that a mesh axis runs over, the one named last changes fastest.
Arguments:
- queries: bfloat16 [2048, 4096], P(('dp', 'seq'), 'mp'), may hold values from -2 to 2
- key_rows: bfloat16 [2048, 4096], P(('dp', 'seq'), 'mp'), may hold values from -2 to 2
- value_rows: bfloat16 [2048, 4096], P(('dp', 'seq'), 'mp'), may hold values from -6 to 6
- row_plan: int32 [4, 4], replicated, may hold values from 0 to 40, as said below
- segments: int32 [4, 512], P('dp', 'seq'), may hold values from 0 to 5, never falling along the last dimension, each value on 1 to 256 neighbouring positions
- norm_gain: float32 [4096], P('mp'), may hold values from 0.5 to 1.5
- out_weight: bfloat16 [4096, 3072], P('mp'), may hold values from -0.09375 to 0.09375
- out_grad: bfloat16 [2048, 3072], P(('dp', 'seq'), 'mp'), may hold values from -6 to 6
Outputs:
- normed: bfloat16 [2048, 4096], P(('dp', 'seq'), 'mp')
- query_grad: bfloat16 [2048, 4096], P(('dp', 'seq'), 'mp')
- key_grad: bfloat16 [2048, 4096], P(('dp', 'seq'), 'mp')
- value_grad: bfloat16 [2048, 4096], P(('dp', 'seq'), 'mp')
- weight_grad: float32 [3072, 4096], P(('dp', 'seq'), 'mp')
The draws below stay inside these ranges and needn't reach their ends.
Inputs may be any that keep to these rules, and one draw needn't show every extreme that they name: Each row and each column of row_plan sums to 128; the plan holds for every sequence shard alike; an arriving group's rows for group 0 come first, then those for group 1, and so on. `segments`: documents never cross data groups.
All inputs are finite; a program needn't handle non-finite values.
Results may differ from the reference program's by a relative error of at most 0.0064.
Values may be sent and summed in bfloat16 or wider, within the bound.
A program may use at most 128 MiB of HBM per device.

```python
import math
import jax
import jax.numpy as jnp
import numpy as np
from jax import lax

HS = 128
HL = 32
DOUT = 3072
ROWS = 128
COUNT = 6
HISTORY = 512
MOST = 256
CAP = 40
TOKENS = 2048
N_DP = 4
N_SEQ = 4


def draw_row_plan(key, part):
    first_key, second_key, third_key, fourth_key = jax.random.split(jax.random.fold_in(key, 17), 4)
    remaining = ROWS - CAP
    shuffled = jax.random.permutation(first_key, (N_DP - 1) * CAP)
    taken = (jnp.arange((N_DP - 1) * CAP) < remaining).astype(jnp.int32)
    bin_index = shuffled // CAP
    rest_weights = jnp.zeros((N_DP - 1,), jnp.int32).at[bin_index].add(taken)
    weights = jnp.concatenate([jnp.full((1,), CAP, jnp.int32), rest_weights])
    weights = weights[jax.random.permutation(second_key, N_DP)]
    source_perm = jax.random.permutation(third_key, N_DP)
    target_perm = jax.random.permutation(fourth_key, N_DP)
    offsets = (target_perm[None, :] - source_perm[:, None]) % N_DP
    return weights[offsets].astype(jnp.int32)


def with_spikes(result, stream_key, source, target, blocks, factor):
    owner, partner = [(jnp.arange(result.shape[position]) // (result.shape[position] // blocks)).reshape([-1 if axis == position else 1 for axis in range(result.ndim)]) for position in (source, target)]
    chosen = jax.random.permutation(stream_key, blocks)[partner]
    strong = (owner == chosen) | (owner == (partner + blocks // 2) % blocks)
    return jnp.where(strong, factor * result, result)


def block_levels(rng, dims, shards, smallest, largest):
    level = 1.0
    for axis_at, shards_of in shards:
        draws = jax.random.uniform(jax.random.fold_in(jax.random.fold_in(rng, 6), axis_at), (shards_of,), jnp.float32, smallest / len(shards), largest / len(shards))
        level = level * jnp.repeat(jnp.exp(draws), dims[axis_at] // shards_of).reshape((-1,) + (1,) * (len(dims) - 1 - axis_at))
    return level


def length_profile(count, total, reach, lean):
    loads = [(1 << 20) // math.isqrt(rank ** lean) + 1 for rank in range(2, count + 1)]
    surplus, given = total - reach - (count - 1), [1] * (count - 1)
    while surplus > 0:
        candidates = [i for i in range(count - 1) if given[i] < reach]
        mass, left = sum([loads[i] for i in candidates]), surplus
        for i in candidates:
            more = min(reach - given[i], max(1, left * loads[i] // mass), surplus)
            given[i] = given[i] + more
            surplus = surplus - more
    return np.array([reach] + given)


def ragged_sizes(key, count, total, most, skew):
    if count == 2:
        one = jax.random.randint(key, (), max(1, total - most), min(most, total - 1) + 1)
        return jnp.stack([one, total - one])
    sizes = jnp.asarray(length_profile(count, total, most, skew), jnp.int32)
    couples = (count - 1) // 2
    giver, receiver = sizes[1:1 + 2 * couples:2], sizes[2:2 + 2 * couples:2]
    room = jnp.minimum(giver - 1, most - receiver)
    moved = jax.random.randint(jax.random.fold_in(key, 1), (couples,), 0, 1 << 20) % (room + 1)
    sizes = sizes.at[1:1 + 2 * couples:2].set(giver - moved).at[2:2 + 2 * couples:2].set(receiver + moved)
    return sizes[jax.random.permutation(jax.random.fold_in(key, 2), count)]


def scatter_about(rng, shape, spread, most, cuts=(), kind=jnp.bfloat16):
    entries = jax.random.normal(rng, shape, jnp.float32) * spread
    if len(cuts) > 0:
        entries = block_levels(rng, shape, cuts, -0.22, 0.18) * entries
    return jnp.clip(entries, min=-most, max=most).astype(kind)


def noise_with(key, shape, spread, bound, shards, heavy, kind=jnp.bfloat16):
    result = spread * jax.random.normal(key, shape, jnp.float32)
    if shards:
        result = result * block_levels(key, shape, shards, -0.22, 0.18)
    return jnp.clip(with_spikes(result, jax.random.fold_in(key, 3), *heavy), -bound, bound).astype(kind)


def setup_inputs(seed: int = 0) -> dict:
    arg_keys = jax.random.split(jax.random.key(seed), 9)
    queries = scatter_about(arg_keys[0], (TOKENS, HL * HS), 0.3, 2.0, ((0, 16), (1, 2)))
    key_rows = scatter_about(arg_keys[1], (TOKENS, HL * HS), 0.3, 2.0, ((0, 16), (1, 2)))
    value_rows = scatter_about(arg_keys[2], (TOKENS, HL * HS), 1.0, 6.0, ((0, 16), (1, 2)))
    row_plan = draw_row_plan(jax.random.fold_in(arg_keys[8], 71), 0)
    segments = jax.vmap(lambda own: jnp.searchsorted(jnp.cumsum(ragged_sizes(own, COUNT, HISTORY, MOST, 2)), jnp.arange(HISTORY), side="right"))(jax.random.split(arg_keys[4], N_DP)).reshape((N_DP, HISTORY)).astype(jnp.int32)
    norm_gain = jnp.clip(0.5 + 1.0 * jax.random.uniform(arg_keys[5], (HL * HS,), jnp.float32) ** block_levels(arg_keys[5], (HL * HS,), ((0, 2),), -0.2, 0.2), 0.5, 1.5)
    out_weight = scatter_about(arg_keys[6], (HL * HS, DOUT), (HL * HS) ** -0.5, 0.09375, ((0, 2),))
    out_grad = noise_with(arg_keys[7], (TOKENS, DOUT), 1.0, 6.0, ((0, 16), (1, 2)), (0, 1, 16, 2.0))
    return dict(queries=queries, key_rows=key_rows, value_rows=value_rows, row_plan=row_plan, segments=segments, norm_gain=norm_gain, out_weight=out_weight, out_grad=out_grad)


NORM_EPS = 1e-06
HIGH = lax.Precision.HIGHEST

def to_half(values):
    return lax.optimization_barrier(values.astype(jnp.bfloat16)).astype(jnp.float32)

def rms_scale(attn, gain_heads):
    power = lax.optimization_barrier(jnp.mean(attn * attn, axis=-1, keepdims=True))
    return attn * lax.rsqrt(power + NORM_EPS) * gain_heads

def route_index(row_plan):
    send_start = jnp.cumsum(row_plan, axis=1) - row_plan
    recv_start = jnp.cumsum(row_plan, axis=0) - row_plan
    recv_end = recv_start + row_plan
    positions = jnp.arange(ROWS, dtype=jnp.int32)
    source = lax.optimization_barrier(jnp.sum((recv_end.T[:, None, :] <= positions[None, :, None]).astype(jnp.int32), axis=2)).astype(jnp.int32)
    target = jnp.arange(N_DP, dtype=jnp.int32)[:, None]
    offset = positions[None, :] - recv_start[source, target] + send_start[source, target]
    return (source, offset.astype(jnp.int32))

def doc_mask(seg_block):
    positions = jnp.arange(seg_block.shape[0], dtype=jnp.int32)
    causal = positions[None, :] <= positions[:, None]
    return (causal & (seg_block[:, None] == seg_block[None, :])).astype(jnp.float32)

def block_forward(carry, block):
    state, last_id = carry
    query, keyv, value, seg_f = block
    same_doc = doc_mask(seg_f)
    scores = to_half(jnp.einsum('thd,shd->hts', query, keyv, precision=HIGH) * same_doc[None])
    inner = jnp.einsum('hts,she->the', scores, value, precision=HIGH)
    carried = (seg_f == last_id).astype(jnp.float32)
    outer = jnp.einsum('thd,hde->the', query, state, precision=HIGH) * carried[:, None, None]
    tail = (seg_f == seg_f[-1]).astype(jnp.float32)
    local_state = jnp.einsum('thd,the->hde', keyv * tail[:, None, None], value, precision=HIGH)
    new_state = local_state + jnp.where(seg_f[-1] == last_id, state, jnp.zeros_like(state))
    return ((new_state, seg_f[-1]), (inner + outer, state, last_id))

def block_backward(carry, block):
    rstate, first_id = carry
    query, keyv, value, seg_f, d_attn, fstate, fid = block
    same_doc = doc_mask(seg_f)
    d_round = to_half(d_attn)
    scores = to_half(jnp.einsum('thd,shd->hts', query, keyv, precision=HIGH) * same_doc[None])
    dprob = to_half(jnp.einsum('the,she->hts', d_round, value, precision=HIGH) * same_doc[None])
    carried = (seg_f == fid).astype(jnp.float32)
    rev_use = (seg_f == first_id).astype(jnp.float32)
    dquery = jnp.einsum('hts,shd->thd', dprob, keyv, precision=HIGH)
    dquery = dquery + jnp.einsum('the,hde->thd', d_attn, fstate, precision=HIGH) * carried[:, None, None]
    dkey = jnp.einsum('hts,thd->shd', dprob, query, precision=HIGH)
    dkey = dkey + jnp.einsum('the,hde->thd', value, rstate, precision=HIGH) * rev_use[:, None, None]
    dvalue = jnp.einsum('hts,the->she', scores, d_round, precision=HIGH)
    dvalue = dvalue + jnp.einsum('thd,hde->the', keyv, rstate, precision=HIGH) * rev_use[:, None, None]
    head_part = (seg_f == seg_f[0]).astype(jnp.float32)
    local_r = jnp.einsum('thd,the->hde', query * head_part[:, None, None], d_attn, precision=HIGH)
    new_r = local_r + jnp.where(seg_f[0] == first_id, rstate, jnp.zeros_like(rstate))
    return ((new_r, seg_f[0]), (dquery, dkey, dvalue))

def reference(queries, key_rows, value_rows, row_plan, segments, norm_gain, out_weight, out_grad):
    width = queries.shape[1]
    heads = width // HS
    source, offset = route_index(row_plan)
    shard_ids = jnp.arange(N_SEQ, dtype=jnp.int32)[None, :, None]

    def reorder(whole):
        split = whole.reshape(N_DP, N_SEQ, ROWS, width)
        return split[source[:, None, :], shard_ids, offset[:, None, :]].reshape(N_DP, N_SEQ * ROWS, width)
    q_all = reorder(queries)
    k_all = reorder(key_rows)
    v_all = reorder(value_rows)
    grad_all = out_grad.reshape(N_DP, N_SEQ * ROWS, DOUT)
    gain_heads = norm_gain.reshape(heads, HS)
    length = N_SEQ * ROWS

    def one_group(weight_acc, group):
        query_g, key_g, value_g, seg_g, grad_g = group
        query = query_g.astype(jnp.float32).reshape(N_SEQ, ROWS, heads, HS)
        keyv = key_g.astype(jnp.float32).reshape(N_SEQ, ROWS, heads, HS)
        value = value_g.astype(jnp.float32).reshape(N_SEQ, ROWS, heads, HS)
        seg_f = seg_g.astype(jnp.float32).reshape(N_SEQ, ROWS)
        start = (jnp.zeros((heads, HS, HS), jnp.float32), jnp.full((), -1.0, jnp.float32))
        _, (attn, fstate, fid) = lax.scan(block_forward, start, (query, keyv, value, seg_f))
        attn_flat = attn.reshape(length, heads, HS)
        normed_f, pull = jax.vjp(lambda a: rms_scale(a, gain_heads), attn_flat)
        normed = normed_f.reshape(length, width).astype(jnp.bfloat16)
        d_normed = lax.dot_general(grad_g, out_weight, (((1,), (1,)), ((), ())), preferred_element_type=jnp.float32)
        d_attn = pull(d_normed.reshape(length, heads, HS))[0]
        d_blocks = d_attn.reshape(N_SEQ, ROWS, heads, HS)
        _, (dquery, dkey, dvalue) = lax.scan(block_backward, start, (query, keyv, value, seg_f, d_blocks, fstate, fid), reverse=True)
        term = lax.dot_general(grad_g, normed, (((0,), (0,)), ((), ())), preferred_element_type=jnp.float32)
        results = (normed, dquery.reshape(length, width).astype(jnp.bfloat16), dkey.reshape(length, width).astype(jnp.bfloat16), dvalue.reshape(length, width).astype(jnp.bfloat16))
        return (weight_acc + term, results)
    weight_grad, (normed, query_grad, key_grad, value_grad) = lax.scan(one_group, jnp.zeros((DOUT, width), jnp.float32), (q_all, k_all, v_all, segments, grad_all))
    total = N_DP * length
    return (normed.reshape(total, width), query_grad.reshape(total, width), key_grad.reshape(total, width), value_grad.reshape(total, width), weight_grad)
```

```python
import functools

import jax
import jax.numpy as jnp
from jax import lax
from jax.experimental import pallas as pl
from jax.experimental.pallas import tpu as pltpu
from jax.sharding import PartitionSpec as P

HS = 128


NORM_EPS = 1e-06
F32 = jnp.float32
BF16 = jnp.bfloat16


def mm(a, b, ca, cb):
    return lax.dot_general(a, b, (((ca,), (cb,)), ((), ())), preferred_element_type=F32)


def place_body(blocks, pick_ref, tail_ref, aq_ref, ak_ref, av_ref, q_ref, k_ref, v_ref, st_ref):
    pick = pick_ref[...]
    tail = tail_ref[...]
    for src, dst in ((aq_ref, q_ref), (ak_ref, k_ref), (av_ref, v_ref)):
        dst[...] = mm(pick, src[...], 1, 0).astype(BF16)
    for h in range(blocks):
        cols = slice(h * HS, (h + 1) * HS)
        st_ref[:, cols] = mm(k_ref[:, cols] * tail, v_ref[:, cols], 0, 0)


def forward_body(
    blocks, doc_ref, carried_ref, headp_ref, gain_ref, q_ref, k_ref, v_ref, st_ref, dn_ref,
    normed_ref, dh_ref, r_ref,
):
    doc = doc_ref[...]
    carried = carried_ref[...]
    headp = headp_ref[...]
    for h in range(blocks):
        cols = slice(h * HS, (h + 1) * HS)
        q, k, v = q_ref[:, cols], k_ref[:, cols], v_ref[:, cols]
        p = (mm(q, k, 1, 1) * doc).astype(BF16)
        attn = mm(p, v, 1, 0) + mm(q, st_ref[:, cols], 1, 0) * carried
        gain = gain_ref[:, cols]
        scale = lax.rsqrt(jnp.mean(attn * attn, axis=-1, keepdims=True) + NORM_EPS)
        unit = attn * scale
        normed_ref[:, cols] = (unit * gain).astype(BF16)
        g = dn_ref[:, cols] * gain
        d_attn = scale * (g - unit * jnp.mean(g * unit, axis=-1, keepdims=True))
        d_half = d_attn.astype(BF16)
        dh_ref[:, cols] = d_half
        r_ref[:, cols] = mm(q * headp, d_half, 0, 0)


def backward_body(
    blocks, doc_ref, carried_ref, rev_ref, q_ref, k_ref, v_ref, d_ref, st_ref, rst_ref,
    dq_ref, dk_ref, dv_ref,
):
    doc = doc_ref[...]
    carried = carried_ref[...]
    rev = rev_ref[...]
    for h in range(blocks):
        cols = slice(h * HS, (h + 1) * HS)
        q, k, v, d = q_ref[:, cols], k_ref[:, cols], v_ref[:, cols], d_ref[:, cols]
        st, rst = st_ref[:, cols], rst_ref[:, cols]
        p = (mm(q, k, 1, 1) * doc).astype(BF16)
        dp = (mm(d, v, 1, 1) * doc).astype(BF16)
        dq_ref[:, cols] = (mm(dp, k, 1, 0) + mm(d, st, 1, 1) * carried).astype(BF16)
        dk_ref[:, cols] = (mm(dp, q, 0, 0) + mm(v, rst, 1, 1) * rev).astype(BF16)
        dv_ref[:, cols] = (mm(p, d, 0, 0) + mm(k, rst, 1, 0) * rev).astype(BF16)


def by_heads(body, heads, fixed, moving, outs):
    blocks = 4 if heads % 4 == 0 else 1
    span = blocks * HS
    rows_of = lambda a: pl.BlockSpec((a.shape[0], span), lambda i: (0, i))
    whole = lambda a: pl.BlockSpec(a.shape, lambda i: (0, 0))
    moved = sum(a.size * a.dtype.itemsize for a in (*fixed, *moving, *outs))
    return pl.pallas_call(
        functools.partial(body, blocks),
        grid=(heads // blocks,),
        in_specs=[whole(a) for a in fixed] + [rows_of(a) for a in moving],
        out_specs=[rows_of(a) for a in outs],
        out_shape=list(outs),
        cost_estimate=pl.CostEstimate(
            flops=16 * heads * HS * HS * HS, bytes_accessed=moved, transcendentals=0
        ),
    )(*fixed, *moving)


def chain(local, ids, axis, reverse):
    peers, place = lax.axis_size(axis), lax.axis_index(axis)
    step = -1 if reverse else 1
    before = jnp.take(ids, jnp.clip(place - step, 0, peers - 1))
    joined = before == jnp.take(ids, place)
    got = jnp.zeros(local.shape, BF16)
    for hop in range(peers - 1):
        at = peers - 1 - hop if reverse else hop
        sent = local if hop == 0 else local + jnp.where(joined, got.astype(F32), 0.0)
        got = got + lax.ppermute(sent.astype(BF16), axis, [(at, at + step)])
    first = place == (peers - 1 if reverse else 0)
    return got, jnp.where(first, jnp.full_like(before, -1.0), before)


def local(queries, key_rows, value_rows, row_plan, segments, norm_gain, out_weight, out_grad):
    row_total = queries.shape[0]
    width = queries.shape[1]
    heads = width // HS
    groups = lax.axis_size("dp")
    my_group = lax.axis_index("dp")
    devices = groups * lax.axis_size("seq")
    capacity = row_total // min(groups, 8) + row_total // 16
    slots_all = groups * capacity
    send_start = jnp.cumsum(row_plan, axis=1) - row_plan
    recv_start = jnp.cumsum(row_plan, axis=0) - row_plan
    slots = jnp.arange(capacity, dtype=jnp.int32)
    positions = jnp.arange(row_total, dtype=jnp.int32)
    my_send = jnp.take(send_start, my_group, axis=0)
    send_index = jnp.minimum(my_send[:, None] + slots[None, :], row_total - 1).reshape(-1)
    send_hot = (send_index[:, None] == positions[None, :]).astype(BF16)

    def hand(x):
        packed = jnp.dot(send_hot, x, preferred_element_type=F32).astype(BF16)
        return lax.all_to_all(packed, "dp", split_axis=0, concat_axis=0, tiled=True)

    arrived = (hand(queries), hand(key_rows), hand(value_rows))
    my_start = jnp.take(recv_start, my_group, axis=1)
    my_end = my_start + jnp.take(row_plan, my_group, axis=1)
    source = jnp.sum((my_end[None, :] <= positions[:, None]).astype(jnp.int32), axis=1)
    pick = source * capacity + positions - jnp.take(my_start, source)
    pick_hot = (pick[:, None] == jnp.arange(slots_all, dtype=jnp.int32)[None, :]).astype(BF16)

    seg_f = segments[0].astype(F32)
    edges = lax.all_gather(jnp.stack([seg_f[0], seg_f[-1]]), "seq")
    causal = positions[None, :] <= positions[:, None]
    same_doc = (causal & (seg_f[:, None] == seg_f[None, :])).astype(F32)
    tail = (seg_f == seg_f[-1]).astype(BF16)[:, None]
    head_part = (seg_f == seg_f[0]).astype(BF16)[:, None]

    full_grad = lax.all_gather(out_grad, "mp", axis=1, tiled=True)
    d_normed = lax.dot_general(
        full_grad, out_weight, (((1,), (1,)), ((), ())), preferred_element_type=F32
    )
    grad_cols = full_grad.T.reshape(devices, full_grad.shape[1] // devices, row_total)
    grad_cols = lax.all_to_all(grad_cols, ("dp", "seq"), split_axis=0, concat_axis=0, tiled=True)

    half = jax.ShapeDtypeStruct((row_total, width), BF16)
    state = jax.ShapeDtypeStruct((HS, width), F32)
    q, k, v, local_state = by_heads(
        place_body, heads, (pick_hot, tail), arrived, (half, half, half, state)
    )
    state_in, id_in = chain(local_state, edges[:, 1], "seq", False)
    carried = (seg_f == id_in).astype(F32)[:, None]
    gain_row = norm_gain.reshape(1, width)
    normed, d_half, local_r = by_heads(
        forward_body,
        heads,
        (same_doc, carried, head_part),
        (gain_row, q, k, v, state_in, d_normed),
        (half, half, state),
    )
    everyone = lax.all_gather(normed, ("dp", "seq"), axis=0)
    rstate_in, rid_in = chain(local_r, edges[:, 0], "seq", True)
    rev_use = (seg_f == rid_in).astype(F32)[:, None]
    dquery, dkey, dvalue = by_heads(
        backward_body,
        heads,
        (same_doc, carried, rev_use),
        (q, k, v, d_half, state_in, rstate_in),
        (half, half, half),
    )
    weight_grad = lax.dot_general(
        grad_cols, everyone, (((0, 2), (0, 1)), ((), ())), preferred_element_type=F32
    )
    return normed, dquery, dkey, dvalue, weight_grad


def solution(mesh):
    placed = (
        P(("dp", "seq"), "mp"),
        P(("dp", "seq"), "mp"),
        P(("dp", "seq"), "mp"),
        P(),
        P("dp", "seq"),
        P("mp"),
        P("mp", None),
        P(("dp", "seq"), "mp"),
    )
    return jax.shard_map(
        local,
        mesh=mesh,
        in_specs=placed,
        out_specs=(
            P(("dp", "seq"), "mp"),
            P(("dp", "seq"), "mp"),
            P(("dp", "seq"), "mp"),
            P(("dp", "seq"), "mp"),
            P(("dp", "seq"), "mp"),
        ),
        check_vma=False,
    )
```

```python
import functools

import jax
import jax.numpy as jnp
from jax import lax
from jax.experimental import pallas as pl
from jax.experimental.pallas import tpu as pltpu
from jax.sharding import PartitionSpec as P

HS = 128


NORM_EPS = 1e-06
F32 = jnp.float32
BF16 = jnp.bfloat16


def mm(a, b, ca, cb):
    return lax.dot_general(a, b, (((ca,), (cb,)), ((), ())), preferred_element_type=F32)


def place_body(blocks, pick_ref, tail_ref, aq_ref, ak_ref, av_ref, q_ref, k_ref, v_ref, st_ref):
    pick = pick_ref[...]
    tail = tail_ref[...]
    for src, dst in ((aq_ref, q_ref), (ak_ref, k_ref), (av_ref, v_ref)):
        dst[...] = mm(pick, src[...], 1, 0).astype(BF16)
    for h in range(blocks):
        cols = slice(h * HS, (h + 1) * HS)
        st_ref[:, cols] = mm(k_ref[:, cols] * tail, v_ref[:, cols], 0, 0)


def forward_body(
    blocks, doc_ref, carried_ref, headp_ref, gain_ref, q_ref, k_ref, v_ref, st_ref, dn_ref,
    normed_ref, dh_ref, r_ref,
):
    doc = doc_ref[...]
    carried = carried_ref[...]
    headp = headp_ref[...]
    for h in range(blocks):
        cols = slice(h * HS, (h + 1) * HS)
        q, k, v = q_ref[:, cols], k_ref[:, cols], v_ref[:, cols]
        p = (mm(q, k, 1, 1) * doc).astype(BF16)
        attn = mm(p, v, 1, 0) + mm(q, st_ref[:, cols], 1, 0) * carried
        gain = gain_ref[:, cols]
        scale = lax.rsqrt(jnp.mean(attn * attn, axis=-1, keepdims=True) + NORM_EPS)
        unit = attn * scale
        normed_ref[:, cols] = (unit * gain).astype(BF16)
        g = dn_ref[:, cols] * gain
        d_attn = scale * (g - unit * jnp.mean(g * unit, axis=-1, keepdims=True))
        d_half = d_attn.astype(BF16)
        dh_ref[:, cols] = d_half
        r_ref[:, cols] = mm(q * headp, d_half, 0, 0)


def backward_body(
    blocks, doc_ref, carried_ref, rev_ref, q_ref, k_ref, v_ref, d_ref, st_ref, rst_ref,
    dq_ref, dk_ref, dv_ref,
):
    doc = doc_ref[...]
    carried = carried_ref[...]
    rev = rev_ref[...]
    for h in range(blocks):
        cols = slice(h * HS, (h + 1) * HS)
        q, k, v, d = q_ref[:, cols], k_ref[:, cols], v_ref[:, cols], d_ref[:, cols]
        st, rst = st_ref[:, cols], rst_ref[:, cols]
        p = (mm(q, k, 1, 1) * doc).astype(BF16)
        dp = (mm(d, v, 1, 1) * doc).astype(BF16)
        dq_ref[:, cols] = (mm(dp, k, 1, 0) + mm(d, st, 1, 1) * carried).astype(BF16)
        dk_ref[:, cols] = (mm(dp, q, 0, 0) + mm(v, rst, 1, 1) * rev).astype(BF16)
        dv_ref[:, cols] = (mm(p, d, 0, 0) + mm(k, rst, 1, 0) * rev).astype(BF16)


def by_heads(body, heads, fixed, moving, outs):
    blocks = 4 if heads % 4 == 0 else 1
    span = blocks * HS
    rows_of = lambda a: pl.BlockSpec((a.shape[0], span), lambda i: (0, i))
    whole = lambda a: pl.BlockSpec(a.shape, lambda i: (0, 0))
    moved = sum(a.size * a.dtype.itemsize for a in (*fixed, *moving, *outs))
    return pl.pallas_call(
        functools.partial(body, blocks),
        grid=(heads // blocks,),
        in_specs=[whole(a) for a in fixed] + [rows_of(a) for a in moving],
        out_specs=[rows_of(a) for a in outs],
        out_shape=list(outs),
        cost_estimate=pl.CostEstimate(
            flops=16 * heads * HS * HS * HS, bytes_accessed=moved, transcendentals=0
        ),
    )(*fixed, *moving)


def gather_body(
    n_z, n_s, grads_ref, normed_ref, local_ref, joined_ref, wg_ref, rst_ref,
    buf, got, sent, zsend, zrecv, xsend, xrecv, csend, crecv, ksend, krecv, own_sem,
):
    n_x = n_s // 2
    z, s = lax.axis_index("dp"), lax.axis_index("seq")
    x, c = lax.div(s, 2), lax.rem(s, 2)
    mate = 2 * x + 1 - c
    width = normed_ref.shape[1]
    span = 512 if width % 512 == 0 else HS

    def remote(src, dst, ssem, rsem, target):
        return pltpu.make_async_remote_copy(
            src_ref=src, dst_ref=dst, send_sem=ssem, recv_sem=rsem,
            device_id=target, device_id_type=pl.DeviceIdType.MESH,
        )

    def zcopy(up, zz, src):
        return remote(src, buf.at[zz, s], zsend.at[0 if up else 1, zz], zrecv.at[zz],
                      {"dp": z + 1 if up else z - 1})

    def xcopy(zz, j, src):
        peer = 2 * lax.rem(x + j, n_x) + c
        return remote(src, buf.at[zz, s], xsend.at[zz, j], xrecv.at[zz, x], {"seq": peer})

    def xland(zz, xs):
        at = buf.at[zz, 2 * xs + c]
        return remote(at, at, xsend.at[zz, 0], xrecv.at[zz, xs], {"seq": 2 * xs + c})

    def ccopy(zz, xs, src):
        return remote(src, buf.at[zz, 2 * xs + c], csend.at[zz, xs], crecv.at[zz, xs],
                      {"seq": mate})

    def cland(zz, xs):
        at = buf.at[zz, 2 * xs + 1 - c]
        return remote(at, at, csend.at[zz, xs], crecv.at[zz, xs], {"seq": mate})

    def kcopy():
        return remote(sent, got, ksend, krecv, {"seq": s - 1})

    greet = [(z > 0, {"dp": z - 1}), (z < n_z - 1, {"dp": z + 1}), (s >= 0, {"seq": mate})]
    greet += [(s >= 0, {"seq": 2 * lax.rem(x + j, n_x) + c}) for j in range(1, n_x)]
    greet += [((c == 0) & (s > 0), {"seq": s - 1}), ((c == 1) & (s < n_s - 1), {"seq": s + 1})]
    barrier = pltpu.get_barrier_semaphore()
    for there, target in greet:
        @pl.when(there)
        def _():
            pl.semaphore_signal(barrier, inc=1, device_id=target,
                                device_id_type=pl.DeviceIdType.MESH)
    pl.semaphore_wait(barrier, sum(jnp.where(there, 1, 0) for there, _ in greet))

    def hand_on(first):
        if first:
            rst_ref[...] = jnp.zeros_like(rst_ref)
            sent[...] = local_ref[...].astype(BF16)
            kcopy().start()
        else:
            kcopy().wait_recv()
            rst_ref[...] = got[...]

            @pl.when(s > 0)
            def _():
                joined = joined_ref[0:1, 0:1]
                sent[...] = (local_ref[...] + got[...].astype(F32) * joined).astype(BF16)
                kcopy().start()

    def level(t):
        if t == 0:
            return ((z >= 0, z),)
        return ((z - t >= 0, z - t), (z + t < n_z, z + t))

    def spread(zz):
        for j in range(1, n_x):
            xs = lax.rem(x + j, n_x)
            xland(zz, xs).wait_recv()
            ccopy(zz, xs, buf.at[zz, 2 * xs + c]).start()

    def add(zz):
        for xs in range(n_x):
            cland(zz, xs).wait_recv()

        def one(sp, carry):
            for at in range(0, width, span):
                cols = slice(at, at + span)
                wg_ref[:, cols] += mm(grads_ref[zz * n_s + sp], buf[zz, sp, :, cols], 1, 0)
            return carry

        lax.fori_loop(0, n_s, one, 0)

    def over(t, act):
        for there, zz in level(t):
            @pl.when(there)
            def _():
                act(zz)

    own = pltpu.make_async_copy(normed_ref, buf.at[z, s], own_sem)
    own.start()

    @pl.when(z < n_z - 1)
    def _():
        zcopy(True, z, normed_ref).start()

    @pl.when(z > 0)
    def _():
        zcopy(False, z, normed_ref).start()

    @pl.when(s == n_s - 1)
    def _():
        hand_on(True)

    ccopy(z, x, normed_ref).start()

    @pl.when((s >= n_s // 2) & (s < n_s - 1))
    def _():
        hand_on(False)

    for j in range(1, n_x):
        xcopy(z, j, normed_ref).start()
    wg_ref[...] = jnp.zeros_like(wg_ref)
    own.wait()

    for t in range(1, n_z):
        for up, (there, zz) in zip((True, False), level(t)):
            @pl.when(there)
            def _():
                block = buf.at[zz, s]
                zcopy(up, zz, block).wait_recv()

                @pl.when((z < n_z - 1) if up else (z > 0))
                def _():
                    zcopy(up, zz, block).start()

                ccopy(zz, x, block).start()
                for j in range(1, n_x):
                    xcopy(zz, j, block).start()
        if t == 1:
            @pl.when(s < n_s // 2)
            def _():
                hand_on(False)
        over(t - 1, spread)
        if t > 1:
            over(t - 2, add)
    over(n_z - 1, spread)
    for t in range(max(n_z - 2, 0), n_z):
        over(t, add)

    def drain(zz):
        for xs in range(n_x):
            ccopy(zz, xs, normed_ref).wait_send()
        for j in range(1, n_x):
            xcopy(zz, j, normed_ref).wait_send()

    for t in range(n_z):
        over(t, drain)
        for up, (there, zz) in zip((True, False), level(t) if t else ((z >= 0, z),) * 2):
            @pl.when(there & ((z < n_z - 1) if up else (z > 0)))
            def _():
                zcopy(up, zz, normed_ref).wait_send()

    @pl.when(s > 0)
    def _():
        kcopy().wait_send()


def gather_grad(grads, normed, local_r, joined, n_z, n_s):
    rows, width = normed.shape
    n_x = n_s // 2
    dma = pltpu.SemaphoreType.DMA
    vmem = pl.BlockSpec(memory_space=pltpu.VMEM)
    return pl.pallas_call(
        functools.partial(gather_body, n_z, n_s),
        out_shape=(
            jax.ShapeDtypeStruct((grads.shape[1], width), F32),
            jax.ShapeDtypeStruct((HS, width), BF16),
        ),
        in_specs=[vmem] * 4,
        out_specs=[vmem] * 2,
        scratch_shapes=[
            pltpu.VMEM((n_z, n_s, rows, width), BF16),
            pltpu.VMEM((HS, width), BF16),
            pltpu.VMEM((HS, width), BF16),
            dma((2, n_z)), dma((n_z,)),
            dma((n_z, n_x)), dma((n_z, n_x)),
            dma((n_z, n_x)), dma((n_z, n_x)),
            dma, dma, dma,
        ],
        compiler_params=pltpu.CompilerParams(collective_id=0, has_side_effects=True),
    )(grads, normed, local_r, joined)


def neighbour(value, axis, step):
    peers, place = lax.axis_size(axis), lax.axis_index(axis)
    pairs = [(i, i + step) for i in range(peers) if 0 <= i + step < peers]
    got = lax.ppermute(jnp.broadcast_to(value, (1, HS)), axis, pairs)[0, 0]
    return jnp.where(place == (0 if step == 1 else peers - 1), -1.0, got)


def chain(local, joined, axis):
    got = jnp.zeros(local.shape, BF16)
    for hop in range(lax.axis_size(axis) - 1):
        sent = local if hop == 0 else local + jnp.where(joined, got.astype(F32), 0.0)
        got = got + lax.ppermute(sent.astype(BF16), axis, [(hop, hop + 1)])
    return got


def whole_rows(part, axis):
    peers, place = lax.axis_size(axis), lax.axis_index(axis)
    rows, cols = part.shape
    full = jnp.zeros((rows, peers * cols), part.dtype)
    full = lax.dynamic_update_slice(full, part, (0, place * cols))
    for j in range(1, peers):
        got = lax.ppermute(part, axis, [(i, (i + j) % peers) for i in range(peers)])
        full = lax.dynamic_update_slice(full, got, (0, lax.rem(place + peers - j, peers) * cols))
    return full


def local(queries, key_rows, value_rows, row_plan, segments, norm_gain, out_weight, out_grad):
    row_total = queries.shape[0]
    width = queries.shape[1]
    heads = width // HS
    groups = lax.axis_size("dp")
    my_group = lax.axis_index("dp")
    devices = groups * lax.axis_size("seq")
    capacity = row_total // min(groups, 8) + row_total // 16
    slots_all = groups * capacity
    send_start = jnp.cumsum(row_plan, axis=1) - row_plan
    recv_start = jnp.cumsum(row_plan, axis=0) - row_plan
    slots = jnp.arange(capacity, dtype=jnp.int32)
    positions = jnp.arange(row_total, dtype=jnp.int32)
    my_send = jnp.take(send_start, my_group, axis=0)
    send_index = jnp.minimum(my_send[:, None] + slots[None, :], row_total - 1).reshape(-1)
    send_hot = (send_index[:, None] == positions[None, :]).astype(BF16)

    def hand(x):
        packed = jnp.dot(send_hot, x, preferred_element_type=F32).astype(BF16)
        return lax.all_to_all(packed, "dp", split_axis=0, concat_axis=0, tiled=True)

    arrived = (hand(queries), hand(key_rows), hand(value_rows))
    my_start = jnp.take(recv_start, my_group, axis=1)
    my_end = my_start + jnp.take(row_plan, my_group, axis=1)
    source = jnp.sum((my_end[None, :] <= positions[:, None]).astype(jnp.int32), axis=1)
    pick = source * capacity + positions - jnp.take(my_start, source)
    pick_hot = (pick[:, None] == jnp.arange(slots_all, dtype=jnp.int32)[None, :]).astype(BF16)

    seg_f = segments[0].astype(F32)
    id_in = neighbour(seg_f[-1], "seq", 1)
    rid_in = neighbour(seg_f[0], "seq", -1)
    causal = positions[None, :] <= positions[:, None]
    same_doc = (causal & (seg_f[:, None] == seg_f[None, :])).astype(F32)
    tail = (seg_f == seg_f[-1]).astype(BF16)[:, None]
    head_part = (seg_f == seg_f[0]).astype(BF16)[:, None]

    full_grad = whole_rows(out_grad, "mp")
    d_normed = lax.dot_general(
        full_grad, out_weight, (((1,), (1,)), ((), ())), preferred_element_type=F32
    )
    grad_cols = full_grad.T.reshape(devices, full_grad.shape[1] // devices, row_total)
    grad_cols = lax.all_to_all(grad_cols, ("dp", "seq"), split_axis=0, concat_axis=0, tiled=True)
    grad_cols, d_normed = lax.optimization_barrier((grad_cols, d_normed))

    half = jax.ShapeDtypeStruct((row_total, width), BF16)
    state = jax.ShapeDtypeStruct((HS, width), F32)
    q, k, v, local_state = by_heads(
        place_body, heads, (pick_hot, tail), arrived, (half, half, half, state)
    )
    state_in = chain(local_state, id_in == seg_f[-1], "seq")
    carried = (seg_f == id_in).astype(F32)[:, None]
    gain_row = norm_gain.reshape(1, width)
    normed, d_half, local_r = by_heads(
        forward_body,
        heads,
        (same_doc, carried, head_part),
        (gain_row, q, k, v, state_in, d_normed),
        (half, half, state),
    )
    rejoined = jnp.broadcast_to((rid_in == seg_f[0]).astype(F32), (8, HS))
    weight_grad, rstate_in = gather_grad(
        grad_cols, normed, local_r, rejoined, groups, lax.axis_size("seq")
    )
    rev_use = (seg_f == rid_in).astype(F32)[:, None]
    dquery, dkey, dvalue = by_heads(
        backward_body,
        heads,
        (same_doc, carried, rev_use),
        (q, k, v, d_half, state_in, rstate_in),
        (half, half, half),
    )
    return normed, dquery, dkey, dvalue, weight_grad


def solution(mesh):
    placed = (
        P(("dp", "seq"), "mp"),
        P(("dp", "seq"), "mp"),
        P(("dp", "seq"), "mp"),
        P(),
        P("dp", "seq"),
        P("mp"),
        P("mp", None),
        P(("dp", "seq"), "mp"),
    )
    return jax.shard_map(
        local,
        mesh=mesh,
        in_specs=placed,
        out_specs=(
            P(("dp", "seq"), "mp"),
            P(("dp", "seq"), "mp"),
            P(("dp", "seq"), "mp"),
            P(("dp", "seq"), "mp"),
            P(("dp", "seq"), "mp"),
        ),
        check_vma=False,
    )
```

```python
import functools

import jax
import jax.numpy as jnp
from jax import lax
from jax.experimental import pallas as pl
from jax.experimental.pallas import tpu as pltpu
from jax.sharding import PartitionSpec as P

HS = 128


NORM_EPS = 1e-06
F32 = jnp.float32
BF16 = jnp.bfloat16


def mm(a, b, ca, cb):
    return lax.dot_general(a, b, (((ca,), (cb,)), ((), ())), preferred_element_type=F32)


def exchange_body(
    n_z, n_m, shot_ref, pick_ref, tail_ref, qi_ref, ki_ref, vi_ref, og_ref, w_ref,
    q_ref, k_ref, v_ref, st_ref, dn_ref, full_ref,
    packed, landed, weight, parts, ssem, rsem, msend, mrecv, wsem,
):
    z, m = lax.axis_index("dp"), lax.axis_index("mp")
    width = qi_ref.shape[1]
    span = 512 if width % 512 == 0 else HS
    fetch = pltpu.make_async_copy(w_ref, weight, wsem)
    fetch.start()
    barrier = pltpu.get_barrier_semaphore()
    peers = [{"mp": lax.rem(m + j, n_m)} for j in range(1, n_m)]
    peers += [{"dp": lax.rem(z + j, n_z)} for j in range(1, n_z)]
    for target in peers:
        pl.semaphore_signal(barrier, inc=1, device_id=target,
                            device_id_type=pl.DeviceIdType.MESH)
    pl.semaphore_wait(barrier, len(peers))

    def mcopy(j, source):
        return pltpu.make_async_remote_copy(
            src_ref=og_ref, dst_ref=parts.at[source], send_sem=msend.at[j],
            recv_sem=mrecv.at[source], device_id={"mp": lax.rem(m + j, n_m)},
            device_id_type=pl.DeviceIdType.MESH,
        )

    def zcopy(a, j, source):
        return pltpu.make_async_remote_copy(
            src_ref=packed.at[a, lax.rem(z + j, n_z)], dst_ref=landed.at[a, source],
            send_sem=ssem.at[a, j], recv_sem=rsem.at[a, source],
            device_id={"dp": lax.rem(z + j, n_z)}, device_id_type=pl.DeviceIdType.MESH,
        )

    for j in range(1, n_m):
        mcopy(j, m).start()
    ins = (ki_ref, vi_ref, qi_ref)
    outs = (k_ref, v_ref, q_ref)
    for a in range(3):
        for j in range(n_z):
            for at in range(0, width, span):
                cols = slice(at, at + span)
                packed[a, j, :, cols] = mm(shot_ref[j], ins[a][:, cols], 1, 0).astype(BF16)
        if a:
            for j in range(1, n_z):
                zcopy(a - 1, j, z).start()
    parts[m] = og_ref[...]
    for a in range(3):
        landed[a, z] = packed[a, z]
    for j in range(1, n_z):
        zcopy(2, j, z).start()

    for j in range(1, n_m):
        mcopy(j, lax.rem(m + j, n_m)).wait_recv()
    full_ref[...] = parts[...]
    fetch.wait()
    part = og_ref.shape[1]

    def block(i, carry):
        total = mm(parts[0], weight[i, :, 0:part], 1, 1)
        for j in range(1, n_m):
            total += mm(parts[j], weight[i, :, j * part:(j + 1) * part], 1, 1)
        dn_ref[:, pl.ds(pl.multiple_of(i * HS, HS), HS)] = total
        return carry

    lax.fori_loop(0, width // HS, block, 0)
    tail = tail_ref[...]
    for a in range(3):
        for j in range(1, n_z):
            zcopy(a, j, lax.rem(z + j, n_z)).wait_recv()
        for at in range(0, width, span):
            cols = slice(at, at + span)
            rows = mm(pick_ref[0], landed[a, 0, :, cols], 1, 0)
            for j in range(1, n_z):
                rows += mm(pick_ref[j], landed[a, j, :, cols], 1, 0)
            outs[a][:, cols] = rows.astype(BF16)
        if a == 1:
            for at in range(0, width, HS):
                cols = slice(at, at + HS)
                st_ref[:, cols] = mm(k_ref[:, cols] * tail, v_ref[:, cols], 0, 0)
    for j in range(1, n_m):
        mcopy(j, m).wait_send()
    for a in range(3):
        for j in range(1, n_z):
            zcopy(a, j, z).wait_send()


def exchange(send_hot, pick_hot, tail, queries, key_rows, value_rows, out_grad, weight, n_z, n_m):
    rows, width = queries.shape
    cap = send_hot.shape[1]
    dma = pltpu.SemaphoreType.DMA
    vmem = pl.BlockSpec(memory_space=pltpu.VMEM)
    half = jax.ShapeDtypeStruct((rows, width), BF16)
    weight = weight.reshape(width // HS, HS, weight.shape[1])
    return pl.pallas_call(
        functools.partial(exchange_body, n_z, n_m),
        out_shape=(
            half, half, half,
            jax.ShapeDtypeStruct((HS, width), F32),
            jax.ShapeDtypeStruct((rows, width), F32),
            jax.ShapeDtypeStruct((n_m, *out_grad.shape), BF16),
        ),
        in_specs=[vmem] * 7 + [pl.BlockSpec(memory_space=pl.ANY)],
        out_specs=[vmem] * 6,
        scratch_shapes=[
            pltpu.VMEM((3, n_z, cap, width), BF16),
            pltpu.VMEM((3, n_z, cap, width), BF16),
            pltpu.VMEM(weight.shape, BF16),
            pltpu.VMEM((n_m, *out_grad.shape), BF16),
            dma((3, n_z)), dma((3, n_z)), dma((n_m,)), dma((n_m,)), dma,
        ],
        compiler_params=pltpu.CompilerParams(collective_id=1, has_side_effects=True),
    )(send_hot, pick_hot, tail, queries, key_rows, value_rows, out_grad, weight)


def forward_body(
    blocks, doc_ref, carried_ref, headp_ref, gain_ref, q_ref, k_ref, v_ref, st_ref, dn_ref,
    normed_ref, dh_ref, r_ref,
):
    doc = doc_ref[...]
    carried = carried_ref[...]
    headp = headp_ref[...]
    for h in range(blocks):
        cols = slice(h * HS, (h + 1) * HS)
        q, k, v = q_ref[:, cols], k_ref[:, cols], v_ref[:, cols]
        p = (mm(q, k, 1, 1) * doc).astype(BF16)
        attn = mm(p, v, 1, 0) + mm(q, st_ref[:, cols], 1, 0) * carried
        gain = gain_ref[:, cols]
        scale = lax.rsqrt(jnp.mean(attn * attn, axis=-1, keepdims=True) + NORM_EPS)
        unit = attn * scale
        normed_ref[:, cols] = (unit * gain).astype(BF16)
        g = dn_ref[:, cols] * gain
        d_attn = scale * (g - unit * jnp.mean(g * unit, axis=-1, keepdims=True))
        d_half = d_attn.astype(BF16)
        dh_ref[:, cols] = d_half
        r_ref[:, cols] = mm(q * headp, d_half, 0, 0)


def backward_body(
    blocks, doc_ref, carried_ref, rev_ref, q_ref, k_ref, v_ref, d_ref, st_ref, rst_ref,
    dq_ref, dk_ref, dv_ref,
):
    doc = doc_ref[...]
    carried = carried_ref[...]
    rev = rev_ref[...]
    for h in range(blocks):
        cols = slice(h * HS, (h + 1) * HS)
        q, k, v, d = q_ref[:, cols], k_ref[:, cols], v_ref[:, cols], d_ref[:, cols]
        st, rst = st_ref[:, cols], rst_ref[:, cols]
        p = (mm(q, k, 1, 1) * doc).astype(BF16)
        dp = (mm(d, v, 1, 1) * doc).astype(BF16)
        dq_ref[:, cols] = (mm(dp, k, 1, 0) + mm(d, st, 1, 1) * carried).astype(BF16)
        dk_ref[:, cols] = (mm(dp, q, 0, 0) + mm(v, rst, 1, 1) * rev).astype(BF16)
        dv_ref[:, cols] = (mm(p, d, 0, 0) + mm(k, rst, 1, 0) * rev).astype(BF16)


def by_heads(body, heads, fixed, moving, outs):
    blocks = 4 if heads % 4 == 0 else 1
    span = blocks * HS
    rows_of = lambda a: pl.BlockSpec((a.shape[0], span), lambda i: (0, i))
    whole = lambda a: pl.BlockSpec(a.shape, lambda i: (0, 0))
    moved = sum(a.size * a.dtype.itemsize for a in (*fixed, *moving, *outs))
    return pl.pallas_call(
        functools.partial(body, blocks),
        grid=(heads // blocks,),
        in_specs=[whole(a) for a in fixed] + [rows_of(a) for a in moving],
        out_specs=[rows_of(a) for a in outs],
        out_shape=list(outs),
        cost_estimate=pl.CostEstimate(
            flops=16 * heads * HS * HS * HS, bytes_accessed=moved, transcendentals=0
        ),
    )(*fixed, *moving)


def gather_body(
    n_z, n_s, grads_ref, normed_ref, local_ref, joined_ref, wg_ref, rst_ref,
    buf, got, sent, zsend, zrecv, xsend, xrecv, csend, crecv, ksend, krecv, own_sem,
):
    n_x = n_s // 2
    z, s = lax.axis_index("dp"), lax.axis_index("seq")
    x, c = lax.div(s, 2), lax.rem(s, 2)
    mate = 2 * x + 1 - c
    width = normed_ref.shape[1]
    span = 512 if width % 512 == 0 else HS

    def remote(src, dst, ssem, rsem, target):
        return pltpu.make_async_remote_copy(
            src_ref=src, dst_ref=dst, send_sem=ssem, recv_sem=rsem,
            device_id=target, device_id_type=pl.DeviceIdType.MESH,
        )

    def zcopy(up, zz, src):
        return remote(src, buf.at[zz, s], zsend.at[0 if up else 1, zz], zrecv.at[zz],
                      {"dp": z + 1 if up else z - 1})

    def xcopy(zz, j, src):
        peer = 2 * lax.rem(x + j, n_x) + c
        return remote(src, buf.at[zz, s], xsend.at[zz, j], xrecv.at[zz, x], {"seq": peer})

    def xland(zz, xs):
        at = buf.at[zz, 2 * xs + c]
        return remote(at, at, xsend.at[zz, 0], xrecv.at[zz, xs], {"seq": 2 * xs + c})

    def ccopy(zz, xs, src):
        return remote(src, buf.at[zz, 2 * xs + c], csend.at[zz, xs], crecv.at[zz, xs],
                      {"seq": mate})

    def cland(zz, xs):
        at = buf.at[zz, 2 * xs + 1 - c]
        return remote(at, at, csend.at[zz, xs], crecv.at[zz, xs], {"seq": mate})

    def kcopy():
        return remote(sent, got, ksend, krecv, {"seq": s - 1})

    greet = [(z > 0, {"dp": z - 1}), (z < n_z - 1, {"dp": z + 1}), (s >= 0, {"seq": mate})]
    greet += [(s >= 0, {"seq": 2 * lax.rem(x + j, n_x) + c}) for j in range(1, n_x)]
    greet += [((c == 0) & (s > 0), {"seq": s - 1}), ((c == 1) & (s < n_s - 1), {"seq": s + 1})]
    barrier = pltpu.get_barrier_semaphore()
    for there, target in greet:
        @pl.when(there)
        def _():
            pl.semaphore_signal(barrier, inc=1, device_id=target,
                                device_id_type=pl.DeviceIdType.MESH)
    pl.semaphore_wait(barrier, sum(jnp.where(there, 1, 0) for there, _ in greet))

    def hand_on(first):
        if first:
            rst_ref[...] = jnp.zeros_like(rst_ref)
            sent[...] = local_ref[...].astype(BF16)
            kcopy().start()
        else:
            kcopy().wait_recv()
            rst_ref[...] = got[...]

            @pl.when(s > 0)
            def _():
                joined = joined_ref[0:1, 0:1]
                sent[...] = (local_ref[...] + got[...].astype(F32) * joined).astype(BF16)
                kcopy().start()

    def level(t):
        if t == 0:
            return ((z >= 0, z),)
        return ((z - t >= 0, z - t), (z + t < n_z, z + t))

    def spread(zz):
        for j in range(1, n_x):
            xs = lax.rem(x + j, n_x)
            xland(zz, xs).wait_recv()
            ccopy(zz, xs, buf.at[zz, 2 * xs + c]).start()

    def add(zz):
        for xs in range(n_x):
            cland(zz, xs).wait_recv()

        def one(sp, carry):
            for at in range(0, width, span):
                cols = slice(at, at + span)
                wg_ref[:, cols] += mm(grads_ref[zz * n_s + sp], buf[zz, sp, :, cols], 1, 0)
            return carry

        lax.fori_loop(0, n_s, one, 0)

    def over(t, act):
        for there, zz in level(t):
            @pl.when(there)
            def _():
                act(zz)

    own = pltpu.make_async_copy(normed_ref, buf.at[z, s], own_sem)
    own.start()

    @pl.when(z < n_z - 1)
    def _():
        zcopy(True, z, normed_ref).start()

    @pl.when(z > 0)
    def _():
        zcopy(False, z, normed_ref).start()

    @pl.when(s == n_s - 1)
    def _():
        hand_on(True)

    ccopy(z, x, normed_ref).start()

    @pl.when((s >= n_s // 2) & (s < n_s - 1))
    def _():
        hand_on(False)

    for j in range(1, n_x):
        xcopy(z, j, normed_ref).start()
    wg_ref[...] = jnp.zeros_like(wg_ref)
    own.wait()

    for t in range(1, n_z):
        for up, (there, zz) in zip((True, False), level(t)):
            @pl.when(there)
            def _():
                block = buf.at[zz, s]
                zcopy(up, zz, block).wait_recv()

                @pl.when((z < n_z - 1) if up else (z > 0))
                def _():
                    zcopy(up, zz, block).start()

                ccopy(zz, x, block).start()
                for j in range(1, n_x):
                    xcopy(zz, j, block).start()
        if t == 1:
            @pl.when(s < n_s // 2)
            def _():
                hand_on(False)
        over(t - 1, spread)
        if t > 1:
            over(t - 2, add)
    over(n_z - 1, spread)
    for t in range(max(n_z - 2, 0), n_z):
        over(t, add)

    def drain(zz):
        for xs in range(n_x):
            ccopy(zz, xs, normed_ref).wait_send()
        for j in range(1, n_x):
            xcopy(zz, j, normed_ref).wait_send()

    for t in range(n_z):
        over(t, drain)
        for up, (there, zz) in zip((True, False), level(t) if t else ((z >= 0, z),) * 2):
            @pl.when(there & ((z < n_z - 1) if up else (z > 0)))
            def _():
                zcopy(up, zz, normed_ref).wait_send()

    @pl.when(s > 0)
    def _():
        kcopy().wait_send()


def gather_grad(grads, normed, local_r, joined, n_z, n_s):
    rows, width = normed.shape
    n_x = n_s // 2
    dma = pltpu.SemaphoreType.DMA
    vmem = pl.BlockSpec(memory_space=pltpu.VMEM)
    return pl.pallas_call(
        functools.partial(gather_body, n_z, n_s),
        out_shape=(
            jax.ShapeDtypeStruct((grads.shape[1], width), F32),
            jax.ShapeDtypeStruct((HS, width), BF16),
        ),
        in_specs=[vmem] * 4,
        out_specs=[vmem] * 2,
        scratch_shapes=[
            pltpu.VMEM((n_z, n_s, rows, width), BF16),
            pltpu.VMEM((HS, width), BF16),
            pltpu.VMEM((HS, width), BF16),
            dma((2, n_z)), dma((n_z,)),
            dma((n_z, n_x)), dma((n_z, n_x)),
            dma((n_z, n_x)), dma((n_z, n_x)),
            dma, dma, dma,
        ],
        compiler_params=pltpu.CompilerParams(collective_id=0, has_side_effects=True),
    )(grads, normed, local_r, joined)


def neighbour(value, axis, step):
    peers, place = lax.axis_size(axis), lax.axis_index(axis)
    pairs = [(i, i + step) for i in range(peers) if 0 <= i + step < peers]
    got = lax.ppermute(jnp.broadcast_to(value, (1, HS)), axis, pairs)[0, 0]
    return jnp.where(place == (0 if step == 1 else peers - 1), -1.0, got)


def chain(local, joined, axis):
    got = jnp.zeros(local.shape, BF16)
    for hop in range(lax.axis_size(axis) - 1):
        sent = local if hop == 0 else local + jnp.where(joined, got.astype(F32), 0.0)
        got = got + lax.ppermute(sent.astype(BF16), axis, [(hop, hop + 1)])
    return got


def local(queries, key_rows, value_rows, row_plan, segments, norm_gain, out_weight, out_grad):
    row_total = queries.shape[0]
    width = queries.shape[1]
    heads = width // HS
    groups = lax.axis_size("dp")
    my_group = lax.axis_index("dp")
    devices = groups * lax.axis_size("seq")
    capacity = row_total // min(groups, 8) + row_total // 16
    slots_all = groups * capacity
    send_start = jnp.cumsum(row_plan, axis=1) - row_plan
    recv_start = jnp.cumsum(row_plan, axis=0) - row_plan
    slots = jnp.arange(capacity, dtype=jnp.int32)
    positions = jnp.arange(row_total, dtype=jnp.int32)
    my_send = jnp.take(send_start, my_group, axis=0)
    send_index = jnp.minimum(my_send[:, None] + slots[None, :], row_total - 1).reshape(-1)
    send_hot = (send_index[:, None] == positions[None, :]).astype(BF16)
    send_hot = send_hot.reshape(groups, capacity, row_total)
    my_start = jnp.take(recv_start, my_group, axis=1)
    my_end = my_start + jnp.take(row_plan, my_group, axis=1)
    source = jnp.sum((my_end[None, :] <= positions[:, None]).astype(jnp.int32), axis=1)
    pick = source * capacity + positions - jnp.take(my_start, source)
    all_slots = jnp.arange(slots_all, dtype=jnp.int32).reshape(groups, 1, capacity)
    pick_hot = (pick[None, :, None] == all_slots).astype(BF16)

    seg_f = segments[0].astype(F32)
    id_in = neighbour(seg_f[-1], "seq", 1)
    rid_in = neighbour(seg_f[0], "seq", -1)
    causal = positions[None, :] <= positions[:, None]
    same_doc = (causal & (seg_f[:, None] == seg_f[None, :])).astype(F32)
    tail = (seg_f == seg_f[-1]).astype(BF16)[:, None]
    head_part = (seg_f == seg_f[0]).astype(BF16)[:, None]

    q, k, v, local_state, d_normed, full_grad = exchange(
        send_hot, pick_hot, tail, queries, key_rows, value_rows, out_grad, out_weight,
        groups, lax.axis_size("mp"),
    )
    grad_cols = full_grad.transpose(0, 2, 1).reshape(devices, -1, row_total)
    grad_cols = lax.all_to_all(grad_cols, ("dp", "seq"), split_axis=0, concat_axis=0, tiled=True)

    half = jax.ShapeDtypeStruct((row_total, width), BF16)
    state = jax.ShapeDtypeStruct((HS, width), F32)
    state_in = chain(local_state, id_in == seg_f[-1], "seq")
    carried = (seg_f == id_in).astype(F32)[:, None]
    gain_row = norm_gain.reshape(1, width)
    normed, d_half, local_r = by_heads(
        forward_body,
        heads,
        (same_doc, carried, head_part),
        (gain_row, q, k, v, state_in, d_normed),
        (half, half, state),
    )
    rejoined = jnp.broadcast_to((rid_in == seg_f[0]).astype(F32), (8, HS))
    weight_grad, rstate_in = gather_grad(
        grad_cols, normed, local_r, rejoined, groups, lax.axis_size("seq")
    )
    rev_use = (seg_f == rid_in).astype(F32)[:, None]
    dquery, dkey, dvalue = by_heads(
        backward_body,
        heads,
        (same_doc, carried, rev_use),
        (q, k, v, d_half, state_in, rstate_in),
        (half, half, half),
    )
    return normed, dquery, dkey, dvalue, weight_grad


def solution(mesh):
    placed = (
        P(("dp", "seq"), "mp"),
        P(("dp", "seq"), "mp"),
        P(("dp", "seq"), "mp"),
        P(),
        P("dp", "seq"),
        P("mp"),
        P("mp", None),
        P(("dp", "seq"), "mp"),
    )
    return jax.shard_map(
        local,
        mesh=mesh,
        in_specs=placed,
        out_specs=(
            P(("dp", "seq"), "mp"),
            P(("dp", "seq"), "mp"),
            P(("dp", "seq"), "mp"),
            P(("dp", "seq"), "mp"),
            P(("dp", "seq"), "mp"),
        ),
        check_vma=False,
    )
```

```python
import functools

import jax
import jax.numpy as jnp
from jax import lax
from jax.experimental import pallas as pl
from jax.experimental.pallas import tpu as pltpu
from jax.sharding import PartitionSpec as P

HS = 128


NORM_EPS = 1e-06
F32 = jnp.float32
BF16 = jnp.bfloat16


def mm(a, b, ca, cb):
    return lax.dot_general(a, b, (((ca,), (cb,)), ((), ())), preferred_element_type=F32)


def exchange_body(
    n_z, n_m, shot_ref, pick_ref, tail_ref, qi_ref, ki_ref, vi_ref, og_ref, w_ref,
    q_ref, k_ref, v_ref, st_ref, dn_ref, full_ref,
    packed, landed, weight, parts, ssem, rsem, msend, mrecv, wsem,
):
    z, m = lax.axis_index("dp"), lax.axis_index("mp")
    width = qi_ref.shape[1]
    span = 512 if width % 512 == 0 else HS
    fetch = pltpu.make_async_copy(w_ref, weight, wsem)
    fetch.start()
    barrier = pltpu.get_barrier_semaphore()
    peers = [{"mp": lax.rem(m + j, n_m)} for j in range(1, n_m)]
    peers += [{"dp": lax.rem(z + j, n_z)} for j in range(1, n_z)]
    for target in peers:
        pl.semaphore_signal(barrier, inc=1, device_id=target,
                            device_id_type=pl.DeviceIdType.MESH)
    pl.semaphore_wait(barrier, len(peers))

    def mcopy(j, source):
        return pltpu.make_async_remote_copy(
            src_ref=og_ref, dst_ref=parts.at[source], send_sem=msend.at[j],
            recv_sem=mrecv.at[source], device_id={"mp": lax.rem(m + j, n_m)},
            device_id_type=pl.DeviceIdType.MESH,
        )

    def zcopy(a, j, source):
        return pltpu.make_async_remote_copy(
            src_ref=packed.at[a, lax.rem(z + j, n_z)], dst_ref=landed.at[a, source],
            send_sem=ssem.at[a, j], recv_sem=rsem.at[a, source],
            device_id={"dp": lax.rem(z + j, n_z)}, device_id_type=pl.DeviceIdType.MESH,
        )

    for j in range(1, n_m):
        mcopy(j, m).start()
    ins = (ki_ref, vi_ref, qi_ref)
    outs = (k_ref, v_ref, q_ref)
    for a in range(3):
        for j in range(n_z):
            for at in range(0, width, span):
                cols = slice(at, at + span)
                packed[a, j, :, cols] = mm(shot_ref[j], ins[a][:, cols], 1, 0).astype(BF16)
        if a:
            for j in range(1, n_z):
                zcopy(a - 1, j, z).start()
    parts[m] = og_ref[...]
    for a in range(3):
        landed[a, z] = packed[a, z]
    for j in range(1, n_z):
        zcopy(2, j, z).start()

    for j in range(1, n_m):
        mcopy(j, lax.rem(m + j, n_m)).wait_recv()
    full_ref[...] = parts[...]
    fetch.wait()
    part = og_ref.shape[1]

    def block(i, carry):
        total = mm(parts[0], weight[i, :, 0:part], 1, 1)
        for j in range(1, n_m):
            total += mm(parts[j], weight[i, :, j * part:(j + 1) * part], 1, 1)
        dn_ref[:, pl.ds(pl.multiple_of(i * HS, HS), HS)] = total
        return carry

    lax.fori_loop(0, width // HS, block, 0)
    tail = tail_ref[...]
    for a in range(3):
        for j in range(1, n_z):
            zcopy(a, j, lax.rem(z + j, n_z)).wait_recv()
        for at in range(0, width, span):
            cols = slice(at, at + span)
            rows = mm(pick_ref[0], landed[a, 0, :, cols], 1, 0)
            for j in range(1, n_z):
                rows += mm(pick_ref[j], landed[a, j, :, cols], 1, 0)
            outs[a][:, cols] = rows.astype(BF16)
        if a == 1:
            for at in range(0, width, HS):
                cols = slice(at, at + HS)
                st_ref[:, cols] = mm(k_ref[:, cols] * tail, v_ref[:, cols], 0, 0)
    for j in range(1, n_m):
        mcopy(j, m).wait_send()
    for a in range(3):
        for j in range(1, n_z):
            zcopy(a, j, z).wait_send()


def exchange(send_hot, pick_hot, tail, queries, key_rows, value_rows, out_grad, weight, n_z, n_m):
    rows, width = queries.shape
    cap = send_hot.shape[1]
    dma = pltpu.SemaphoreType.DMA
    vmem = pl.BlockSpec(memory_space=pltpu.VMEM)
    half = jax.ShapeDtypeStruct((rows, width), BF16)
    weight = weight.reshape(width // HS, HS, weight.shape[1])
    return pl.pallas_call(
        functools.partial(exchange_body, n_z, n_m),
        out_shape=(
            half, half, half,
            jax.ShapeDtypeStruct((HS, width), F32),
            jax.ShapeDtypeStruct((rows, width), F32),
            jax.ShapeDtypeStruct((n_m, *out_grad.shape), BF16),
        ),
        in_specs=[vmem] * 7 + [pl.BlockSpec(memory_space=pl.ANY)],
        out_specs=[vmem] * 6,
        scratch_shapes=[
            pltpu.VMEM((3, n_z, cap, width), BF16),
            pltpu.VMEM((3, n_z, cap, width), BF16),
            pltpu.VMEM(weight.shape, BF16),
            pltpu.VMEM((n_m, *out_grad.shape), BF16),
            dma((3, n_z)), dma((3, n_z)), dma((n_m,)), dma((n_m,)), dma,
        ],
        compiler_params=pltpu.CompilerParams(collective_id=1, has_side_effects=True),
    )(send_hot, pick_hot, tail, queries, key_rows, value_rows, out_grad, weight)


def forward_body(
    blocks, doc_ref, carried_ref, headp_ref, gain_ref, q_ref, k_ref, v_ref, st_ref, dn_ref,
    normed_ref, dh_ref, r_ref,
):
    doc = doc_ref[...]
    carried = carried_ref[...]
    headp = headp_ref[...]
    for h in range(blocks):
        cols = slice(h * HS, (h + 1) * HS)
        q, k, v = q_ref[:, cols], k_ref[:, cols], v_ref[:, cols]
        p = (mm(q, k, 1, 1) * doc).astype(BF16)
        attn = mm(p, v, 1, 0) + mm(q, st_ref[:, cols], 1, 0) * carried
        gain = gain_ref[:, cols]
        scale = lax.rsqrt(jnp.mean(attn * attn, axis=-1, keepdims=True) + NORM_EPS)
        unit = attn * scale
        normed_ref[:, cols] = (unit * gain).astype(BF16)
        g = dn_ref[:, cols] * gain
        d_attn = scale * (g - unit * jnp.mean(g * unit, axis=-1, keepdims=True))
        d_half = d_attn.astype(BF16)
        dh_ref[:, cols] = d_half
        r_ref[:, cols] = mm(q * headp, d_half, 0, 0)


def backward_head(cols, doc, carried, rev, refs, dq_ref, dk_ref, dv_ref):
    q, k, v, d, st, rst = (ref[:, cols] for ref in refs)
    p = (mm(q, k, 1, 1) * doc).astype(BF16)
    dp = (mm(d, v, 1, 1) * doc).astype(BF16)
    dq_ref[:, cols] = (mm(dp, k, 1, 0) + mm(d, st, 1, 1) * carried).astype(BF16)
    dk_ref[:, cols] = (mm(dp, q, 0, 0) + mm(v, rst, 1, 1) * rev).astype(BF16)
    dv_ref[:, cols] = (mm(p, d, 0, 0) + mm(k, rst, 1, 0) * rev).astype(BF16)


def by_heads(body, heads, fixed, moving, outs):
    blocks = 4 if heads % 4 == 0 else 1
    span = blocks * HS
    rows_of = lambda a: pl.BlockSpec((a.shape[0], span), lambda i: (0, i))
    whole = lambda a: pl.BlockSpec(a.shape, lambda i: (0, 0))
    moved = sum(a.size * a.dtype.itemsize for a in (*fixed, *moving, *outs))
    return pl.pallas_call(
        functools.partial(body, blocks),
        grid=(heads // blocks,),
        in_specs=[whole(a) for a in fixed] + [rows_of(a) for a in moving],
        out_specs=[rows_of(a) for a in outs],
        out_shape=list(outs),
        cost_estimate=pl.CostEstimate(
            flops=16 * heads * HS * HS * HS, bytes_accessed=moved, transcendentals=0
        ),
    )(*fixed, *moving)


def gather_body(
    n_z, n_s, grads_ref, normed_ref, local_ref, joined_ref,
    doc_ref, carried_ref, rev_ref, q_ref, k_ref, v_ref, d_ref, st_ref,
    wg_ref, dq_ref, dk_ref, dv_ref, rst_ref, buf, got, sent, zsend, zrecv, xsend, xrecv, csend, crecv, ksend, krecv, own_sem,
):
    n_x = n_s // 2
    z, s = lax.axis_index("dp"), lax.axis_index("seq")
    x, c = lax.div(s, 2), lax.rem(s, 2)
    mate = 2 * x + 1 - c
    width = normed_ref.shape[1]
    span = 512 if width % 512 == 0 else HS

    def remote(src, dst, ssem, rsem, target):
        return pltpu.make_async_remote_copy(
            src_ref=src, dst_ref=dst, send_sem=ssem, recv_sem=rsem,
            device_id=target, device_id_type=pl.DeviceIdType.MESH,
        )

    def zcopy(up, zz, src):
        return remote(src, buf.at[zz, s], zsend.at[0 if up else 1, zz], zrecv.at[zz],
                      {"dp": z + 1 if up else z - 1})

    def xcopy(zz, j, src):
        peer = 2 * lax.rem(x + j, n_x) + c
        return remote(src, buf.at[zz, s], xsend.at[zz, j], xrecv.at[zz, x], {"seq": peer})

    def xland(zz, xs):
        at = buf.at[zz, 2 * xs + c]
        return remote(at, at, xsend.at[zz, 0], xrecv.at[zz, xs], {"seq": 2 * xs + c})

    def ccopy(zz, xs, src):
        return remote(src, buf.at[zz, 2 * xs + c], csend.at[zz, xs], crecv.at[zz, xs],
                      {"seq": mate})

    def cland(zz, xs):
        at = buf.at[zz, 2 * xs + 1 - c]
        return remote(at, at, csend.at[zz, xs], crecv.at[zz, xs], {"seq": mate})

    def kcopy():
        return remote(sent, got, ksend, krecv, {"seq": s - 1})

    greet = [(z > 0, {"dp": z - 1}), (z < n_z - 1, {"dp": z + 1}), (s >= 0, {"seq": mate})]
    greet += [(s >= 0, {"seq": 2 * lax.rem(x + j, n_x) + c}) for j in range(1, n_x)]
    greet += [((c == 0) & (s > 0), {"seq": s - 1}), ((c == 1) & (s < n_s - 1), {"seq": s + 1})]
    barrier = pltpu.get_barrier_semaphore()
    for there, target in greet:
        @pl.when(there)
        def _():
            pl.semaphore_signal(barrier, inc=1, device_id=target,
                                device_id_type=pl.DeviceIdType.MESH)
    pl.semaphore_wait(barrier, sum(jnp.where(there, 1, 0) for there, _ in greet))

    def hand_on(first):
        if first:
            rst_ref[...] = jnp.zeros_like(rst_ref)
            sent[...] = local_ref[...].astype(BF16)
            kcopy().start()
        else:
            kcopy().wait_recv()
            rst_ref[...] = got[...]

            @pl.when(s > 0)
            def _():
                joined = joined_ref[0:1, 0:1]
                sent[...] = (local_ref[...] + got[...].astype(F32) * joined).astype(BF16)
                kcopy().start()

    def level(t):
        if t == 0:
            return ((z >= 0, z),)
        return ((z - t >= 0, z - t), (z + t < n_z, z + t))

    def spread(zz):
        for j in range(1, n_x):
            xs = lax.rem(x + j, n_x)
            xland(zz, xs).wait_recv()
            ccopy(zz, xs, buf.at[zz, 2 * xs + c]).start()

    def add(zz):
        for xs in range(n_x):
            cland(zz, xs).wait_recv()

        def one(sp, carry):
            for at in range(0, width, span):
                cols = slice(at, at + span)
                wg_ref[:, cols] += mm(grads_ref[zz * n_s + sp], buf[zz, sp, :, cols], 1, 0)
            return carry

        lax.fori_loop(0, n_s, one, 0)

    def over(t, act):
        for there, zz in level(t):
            @pl.when(there)
            def _():
                act(zz)

    own = pltpu.make_async_copy(normed_ref, buf.at[z, s], own_sem)
    own.start()

    @pl.when(z < n_z - 1)
    def _():
        zcopy(True, z, normed_ref).start()

    @pl.when(z > 0)
    def _():
        zcopy(False, z, normed_ref).start()

    @pl.when(s == n_s - 1)
    def _():
        hand_on(True)

    ccopy(z, x, normed_ref).start()

    @pl.when((s >= n_s // 2) & (s < n_s - 1))
    def _():
        hand_on(False)

    for j in range(1, n_x):
        xcopy(z, j, normed_ref).start()
    wg_ref[...] = jnp.zeros_like(wg_ref)
    own.wait()

    for t in range(1, n_z):
        for up, (there, zz) in zip((True, False), level(t)):
            @pl.when(there)
            def _():
                block = buf.at[zz, s]
                zcopy(up, zz, block).wait_recv()

                @pl.when((z < n_z - 1) if up else (z > 0))
                def _():
                    zcopy(up, zz, block).start()

                ccopy(zz, x, block).start()
                for j in range(1, n_x):
                    xcopy(zz, j, block).start()
        if t == 1:
            @pl.when(s < n_s // 2)
            def _():
                hand_on(False)
        over(t - 1, spread)
        if t > 1:
            over(t - 2, add)
    def heads_at(i, carry):
        doc, carried, rev = doc_ref[...], carried_ref[...], rev_ref[...]
        for h in range(blocks):
            cols = pl.ds(pl.multiple_of((i * blocks + h) * HS, HS), HS)
            backward_head(cols, doc, carried, rev, (q_ref, k_ref, v_ref, d_ref, st_ref, rst_ref),
                          dq_ref, dk_ref, dv_ref)
        return carry

    blocks = 4 if width % (4 * HS) == 0 else 1
    lax.fori_loop(0, width // (blocks * HS), heads_at, 0)
    over(n_z - 1, spread)
    for t in range(max(n_z - 2, 0), n_z):
        over(t, add)

    def drain(zz):
        for xs in range(n_x):
            ccopy(zz, xs, normed_ref).wait_send()
        for j in range(1, n_x):
            xcopy(zz, j, normed_ref).wait_send()

    for t in range(n_z):
        over(t, drain)
        for up, (there, zz) in zip((True, False), level(t) if t else ((z >= 0, z),) * 2):
            @pl.when(there & ((z < n_z - 1) if up else (z > 0)))
            def _():
                zcopy(up, zz, normed_ref).wait_send()

    @pl.when(s > 0)
    def _():
        kcopy().wait_send()


def gather_grad(grads, normed, local_r, joined, others, n_z, n_s):
    rows, width = normed.shape
    n_x = n_s // 2
    dma = pltpu.SemaphoreType.DMA
    vmem = pl.BlockSpec(memory_space=pltpu.VMEM)
    return pl.pallas_call(
        functools.partial(gather_body, n_z, n_s),
        out_shape=(
            jax.ShapeDtypeStruct((grads.shape[1], width), F32),
            *[jax.ShapeDtypeStruct((rows, width), BF16)] * 3,
        ),
        in_specs=[vmem] * (4 + len(others)),
        out_specs=[vmem] * 4,
        scratch_shapes=[
            pltpu.VMEM((HS, width), BF16),
            pltpu.VMEM((n_z, n_s, rows, width), BF16),
            pltpu.VMEM((HS, width), BF16),
            pltpu.VMEM((HS, width), BF16),
            dma((2, n_z)), dma((n_z,)),
            dma((n_z, n_x)), dma((n_z, n_x)),
            dma((n_z, n_x)), dma((n_z, n_x)),
            dma, dma, dma,
        ],
        compiler_params=pltpu.CompilerParams(collective_id=0, has_side_effects=True),
    )(grads, normed, local_r, joined, *others)


def neighbour(value, axis, step):
    peers, place = lax.axis_size(axis), lax.axis_index(axis)
    pairs = [(i, i + step) for i in range(peers) if 0 <= i + step < peers]
    got = lax.ppermute(jnp.broadcast_to(value, (1, HS)), axis, pairs)[0, 0]
    return jnp.where(place == (0 if step == 1 else peers - 1), -1.0, got)


def chain(local, joined, axis):
    got = jnp.zeros(local.shape, BF16)
    for hop in range(lax.axis_size(axis) - 1):
        sent = local if hop == 0 else local + jnp.where(joined, got.astype(F32), 0.0)
        got = got + lax.ppermute(sent.astype(BF16), axis, [(hop, hop + 1)])
    return got


def local(queries, key_rows, value_rows, row_plan, segments, norm_gain, out_weight, out_grad):
    row_total = queries.shape[0]
    width = queries.shape[1]
    heads = width // HS
    groups = lax.axis_size("dp")
    my_group = lax.axis_index("dp")
    devices = groups * lax.axis_size("seq")
    capacity = row_total // min(groups, 8) + row_total // 16
    groups_at = jnp.arange(groups, dtype=jnp.int32)
    below = (groups_at[:, None] < groups_at[None, :]).astype(jnp.int32)
    mine = (groups_at == my_group).astype(jnp.int32)
    to_others = jnp.sum(row_plan * mine[:, None], axis=0)
    to_me = jnp.sum(row_plan * mine[None, :], axis=1)
    my_send = jnp.sum(to_others[:, None] * below, axis=0)
    my_start = jnp.sum(to_me[:, None] * below, axis=0)
    slots = jnp.arange(capacity, dtype=jnp.int32)
    positions = jnp.arange(row_total, dtype=jnp.int32)
    send_index = jnp.minimum(my_send[:, None] + slots[None, :], row_total - 1)
    send_hot = (send_index[:, :, None] == positions[None, None, :]).astype(BF16)
    placed = positions[None, :, None] - my_start[:, None, None] == slots[None, None, :]
    pick_hot = (placed & (slots[None, None, :] < to_me[:, None, None])).astype(BF16)

    seg_f = segments[0].astype(F32)
    id_in = neighbour(seg_f[-1], "seq", 1)
    rid_in = neighbour(seg_f[0], "seq", -1)
    causal = positions[None, :] <= positions[:, None]
    same_doc = (causal & (seg_f[:, None] == seg_f[None, :])).astype(F32)
    tail = (seg_f == seg_f[-1]).astype(BF16)[:, None]
    head_part = (seg_f == seg_f[0]).astype(BF16)[:, None]

    q, k, v, local_state, d_normed, full_grad = exchange(
        send_hot, pick_hot, tail, queries, key_rows, value_rows, out_grad, out_weight,
        groups, lax.axis_size("mp"),
    )
    grad_cols = full_grad.transpose(0, 2, 1).reshape(devices, -1, row_total)
    grad_cols = lax.all_to_all(grad_cols, ("dp", "seq"), split_axis=0, concat_axis=0, tiled=True)

    half = jax.ShapeDtypeStruct((row_total, width), BF16)
    state = jax.ShapeDtypeStruct((HS, width), F32)
    state_in = chain(local_state, id_in == seg_f[-1], "seq")
    carried = (seg_f == id_in).astype(F32)[:, None]
    gain_row = norm_gain.reshape(1, width)
    normed, d_half, local_r = by_heads(
        forward_body,
        heads,
        (same_doc, carried, head_part),
        (gain_row, q, k, v, state_in, d_normed),
        (half, half, state),
    )
    rejoined = jnp.broadcast_to((rid_in == seg_f[0]).astype(F32), (8, HS))
    rev_use = (seg_f == rid_in).astype(F32)[:, None]
    others = (same_doc, carried, rev_use, q, k, v, d_half, state_in)
    weight_grad, dquery, dkey, dvalue = gather_grad(
        grad_cols, normed, local_r, rejoined, others, groups, lax.axis_size("seq")
    )
    return normed, dquery, dkey, dvalue, weight_grad


def solution(mesh):
    placed = (
        P(("dp", "seq"), "mp"),
        P(("dp", "seq"), "mp"),
        P(("dp", "seq"), "mp"),
        P(),
        P("dp", "seq"),
        P("mp"),
        P("mp", None),
        P(("dp", "seq"), "mp"),
    )
    return jax.shard_map(
        local,
        mesh=mesh,
        in_specs=placed,
        out_specs=(
            P(("dp", "seq"), "mp"),
            P(("dp", "seq"), "mp"),
            P(("dp", "seq"), "mp"),
            P(("dp", "seq"), "mp"),
            P(("dp", "seq"), "mp"),
        ),
        check_vma=False,
    )
```

```python
import functools

import jax
import jax.numpy as jnp
from jax import lax
from jax.experimental import pallas as pl
from jax.experimental.pallas import tpu as pltpu
from jax.sharding import PartitionSpec as P

HS = 128


NORM_EPS = 1e-06
F32 = jnp.float32
BF16 = jnp.bfloat16


def mm(a, b, ca, cb):
    return lax.dot_general(a, b, (((ca,), (cb,)), ((), ())), preferred_element_type=F32)


def exchange_body(
    n_z, n_m, shot_ref, pick_ref, tail_ref, qi_ref, ki_ref, vi_ref, og_ref, w_ref,
    q_ref, k_ref, v_ref, st_ref, dn_ref, full_ref,
    packed, landed, weight, parts, ssem, rsem, msend, mrecv, wsem,
):
    z, m = lax.axis_index("dp"), lax.axis_index("mp")
    width = qi_ref.shape[1]
    span = 512 if width % 512 == 0 else HS
    fetch = pltpu.make_async_copy(w_ref, weight, wsem)
    fetch.start()
    barrier = pltpu.get_barrier_semaphore()
    peers = [{"mp": lax.rem(m + j, n_m)} for j in range(1, n_m)]
    peers += [{"dp": lax.rem(z + j, n_z)} for j in range(1, n_z)]
    for target in peers:
        pl.semaphore_signal(barrier, inc=1, device_id=target,
                            device_id_type=pl.DeviceIdType.MESH)
    pl.semaphore_wait(barrier, len(peers))

    def mcopy(j, source):
        return pltpu.make_async_remote_copy(
            src_ref=og_ref, dst_ref=parts.at[source], send_sem=msend.at[j],
            recv_sem=mrecv.at[source], device_id={"mp": lax.rem(m + j, n_m)},
            device_id_type=pl.DeviceIdType.MESH,
        )

    def zcopy(a, j, source):
        return pltpu.make_async_remote_copy(
            src_ref=packed.at[a, lax.rem(z + j, n_z)], dst_ref=landed.at[a, source],
            send_sem=ssem.at[a, j], recv_sem=rsem.at[a, source],
            device_id={"dp": lax.rem(z + j, n_z)}, device_id_type=pl.DeviceIdType.MESH,
        )

    for j in range(1, n_m):
        mcopy(j, m).start()
    ins = (ki_ref, vi_ref, qi_ref)
    outs = (k_ref, v_ref, q_ref)
    for a in range(3):
        for j in range(n_z):
            for at in range(0, width, span):
                cols = slice(at, at + span)
                packed[a, j, :, cols] = mm(shot_ref[j], ins[a][:, cols], 1, 0).astype(BF16)
        if a:
            for j in range(1, n_z):
                zcopy(a - 1, j, z).start()
    parts[m] = og_ref[...]
    for a in range(3):
        landed[a, z] = packed[a, z]
    for j in range(1, n_z):
        zcopy(2, j, z).start()

    for j in range(1, n_m):
        mcopy(j, lax.rem(m + j, n_m)).wait_recv()
    full_ref[...] = parts[...]
    fetch.wait()
    part = og_ref.shape[1]

    def block(i, carry):
        total = mm(parts[0], weight[i, :, 0:part], 1, 1)
        for j in range(1, n_m):
            total += mm(parts[j], weight[i, :, j * part:(j + 1) * part], 1, 1)
        dn_ref[:, pl.ds(pl.multiple_of(i * HS, HS), HS)] = total
        return carry

    lax.fori_loop(0, width // HS, block, 0)
    tail = tail_ref[...]
    for a in range(3):
        for j in range(1, n_z):
            zcopy(a, j, lax.rem(z + j, n_z)).wait_recv()
        for at in range(0, width, span):
            cols = slice(at, at + span)
            rows = mm(pick_ref[0], landed[a, 0, :, cols], 1, 0)
            for j in range(1, n_z):
                rows += mm(pick_ref[j], landed[a, j, :, cols], 1, 0)
            outs[a][:, cols] = rows.astype(BF16)
        if a == 1:
            for at in range(0, width, HS):
                cols = slice(at, at + HS)
                st_ref[:, cols] = mm(k_ref[:, cols] * tail, v_ref[:, cols], 0, 0)
    for j in range(1, n_m):
        mcopy(j, m).wait_send()
    for a in range(3):
        for j in range(1, n_z):
            zcopy(a, j, z).wait_send()


def exchange(send_hot, pick_hot, tail, queries, key_rows, value_rows, out_grad, weight, n_z, n_m):
    rows, width = queries.shape
    cap = send_hot.shape[1]
    dma = pltpu.SemaphoreType.DMA
    vmem = pl.BlockSpec(memory_space=pltpu.VMEM)
    half = jax.ShapeDtypeStruct((rows, width), BF16)
    weight = weight.reshape(width // HS, HS, weight.shape[1])
    return pl.pallas_call(
        functools.partial(exchange_body, n_z, n_m),
        out_shape=(
            half, half, half,
            jax.ShapeDtypeStruct((HS, width), F32),
            jax.ShapeDtypeStruct((rows, width), F32),
            jax.ShapeDtypeStruct((n_m, *out_grad.shape), BF16),
        ),
        in_specs=[vmem] * 7 + [pl.BlockSpec(memory_space=pl.ANY)],
        out_specs=[vmem] * 6,
        scratch_shapes=[
            pltpu.VMEM((3, n_z, cap, width), BF16),
            pltpu.VMEM((3, n_z, cap, width), BF16),
            pltpu.VMEM(weight.shape, BF16),
            pltpu.VMEM((n_m, *out_grad.shape), BF16),
            dma((3, n_z)), dma((3, n_z)), dma((n_m,)), dma((n_m,)), dma,
        ],
        compiler_params=pltpu.CompilerParams(collective_id=1, has_side_effects=True),
    )(send_hot, pick_hot, tail, queries, key_rows, value_rows, out_grad, weight)


def forward_body(
    blocks, doc_ref, carried_ref, headp_ref, gain_ref, q_ref, k_ref, v_ref, st_ref, dn_ref,
    normed_ref, dh_ref, r_ref,
):
    doc = doc_ref[...]
    carried = carried_ref[...]
    headp = headp_ref[...]
    for h in range(blocks):
        cols = slice(h * HS, (h + 1) * HS)
        q, k, v = q_ref[:, cols], k_ref[:, cols], v_ref[:, cols]
        p = (mm(q, k, 1, 1) * doc).astype(BF16)
        attn = mm(p, v, 1, 0) + mm(q, st_ref[:, cols], 1, 0) * carried
        gain = gain_ref[:, cols]
        scale = lax.rsqrt(jnp.mean(attn * attn, axis=-1, keepdims=True) + NORM_EPS)
        unit = attn * scale
        normed_ref[:, cols] = (unit * gain).astype(BF16)
        g = dn_ref[:, cols] * gain
        d_attn = scale * (g - unit * jnp.mean(g * unit, axis=-1, keepdims=True))
        d_half = d_attn.astype(BF16)
        dh_ref[:, cols] = d_half
        r_ref[:, cols] = mm(q * headp, d_half, 0, 0)


def backward_head(cols, doc, carried, rev, refs, dq_ref, dk_ref, dv_ref):
    q, k, v, d, st, rst = (ref[:, cols] for ref in refs)
    p = (mm(q, k, 1, 1) * doc).astype(BF16)
    dp = (mm(d, v, 1, 1) * doc).astype(BF16)
    dq_ref[:, cols] = (mm(dp, k, 1, 0) + mm(d, st, 1, 1) * carried).astype(BF16)
    dk_ref[:, cols] = (mm(dp, q, 0, 0) + mm(v, rst, 1, 1) * rev).astype(BF16)
    dv_ref[:, cols] = (mm(p, d, 0, 0) + mm(k, rst, 1, 0) * rev).astype(BF16)


def by_heads(body, heads, fixed, moving, outs):
    blocks = 4 if heads % 4 == 0 else 1
    span = blocks * HS
    rows_of = lambda a: pl.BlockSpec((a.shape[0], span), lambda i: (0, i))
    whole = lambda a: pl.BlockSpec(a.shape, lambda i: (0, 0))
    moved = sum(a.size * a.dtype.itemsize for a in (*fixed, *moving, *outs))
    return pl.pallas_call(
        functools.partial(body, blocks),
        grid=(heads // blocks,),
        in_specs=[whole(a) for a in fixed] + [rows_of(a) for a in moving],
        out_specs=[rows_of(a) for a in outs],
        out_shape=list(outs),
        cost_estimate=pl.CostEstimate(
            flops=16 * heads * HS * HS * HS, bytes_accessed=moved, transcendentals=0
        ),
    )(*fixed, *moving)


def gather_body(
    n_z, n_s, grads_ref, normed_ref, local_ref, joined_ref,
    doc_ref, carried_ref, rev_ref, q_ref, k_ref, v_ref, d_ref, st_ref,
    wg_ref, dq_ref, dk_ref, dv_ref, rst_ref, buf, got, sent, zsend, zrecv, xsend, xrecv, csend, crecv, ksend, krecv, own_sem,
):
    n_x = n_s // 2
    z, s = lax.axis_index("dp"), lax.axis_index("seq")
    x, c = lax.div(s, 2), lax.rem(s, 2)
    mate = 2 * x + 1 - c
    width = normed_ref.shape[1]
    span = 512 if width % 512 == 0 else HS

    def remote(src, dst, ssem, rsem, target):
        return pltpu.make_async_remote_copy(
            src_ref=src, dst_ref=dst, send_sem=ssem, recv_sem=rsem,
            device_id=target, device_id_type=pl.DeviceIdType.MESH,
        )

    def zcopy(up, zz, src):
        return remote(src, buf.at[zz, s], zsend.at[0 if up else 1, zz], zrecv.at[zz],
                      {"dp": z + 1 if up else z - 1})

    def xcopy(zz, j, src):
        peer = 2 * lax.rem(x + j, n_x) + c
        return remote(src, buf.at[zz, s], xsend.at[zz, j], xrecv.at[zz, x], {"seq": peer})

    def xland(zz, xs):
        at = buf.at[zz, 2 * xs + c]
        return remote(at, at, xsend.at[zz, 0], xrecv.at[zz, xs], {"seq": 2 * xs + c})

    def ccopy(zz, xs, src):
        return remote(src, buf.at[zz, 2 * xs + c], csend.at[zz, xs], crecv.at[zz, xs],
                      {"seq": mate})

    def cland(zz, xs):
        at = buf.at[zz, 2 * xs + 1 - c]
        return remote(at, at, csend.at[zz, xs], crecv.at[zz, xs], {"seq": mate})

    def kcopy():
        return remote(sent, got, ksend, krecv, {"seq": s - 1})

    greet = [(z > 0, {"dp": z - 1}), (z < n_z - 1, {"dp": z + 1}), (s >= 0, {"seq": mate})]
    greet += [(s >= 0, {"seq": 2 * lax.rem(x + j, n_x) + c}) for j in range(1, n_x)]
    greet += [((c == 0) & (s > 0), {"seq": s - 1}), ((c == 1) & (s < n_s - 1), {"seq": s + 1})]
    barrier = pltpu.get_barrier_semaphore()
    for there, target in greet:
        @pl.when(there)
        def _():
            pl.semaphore_signal(barrier, inc=1, device_id=target,
                                device_id_type=pl.DeviceIdType.MESH)
    pl.semaphore_wait(barrier, sum(jnp.where(there, 1, 0) for there, _ in greet))

    def hand_on(first):
        if first:
            rst_ref[...] = jnp.zeros_like(rst_ref)
            sent[...] = local_ref[...].astype(BF16)
            kcopy().start()
        else:
            kcopy().wait_recv()
            rst_ref[...] = got[...]

            @pl.when(s > 0)
            def _():
                joined = joined_ref[0:1, 0:1]
                sent[...] = (local_ref[...] + got[...].astype(F32) * joined).astype(BF16)
                kcopy().start()

    def level(t):
        if t == 0:
            return ((z >= 0, z),)
        return ((z - t >= 0, z - t), (z + t < n_z, z + t))

    def spread(zz):
        for j in range(1, n_x):
            xs = lax.rem(x + j, n_x)
            xland(zz, xs).wait_recv()
            ccopy(zz, xs, buf.at[zz, 2 * xs + c]).start()

    def add(zz):
        for xs in range(n_x):
            cland(zz, xs).wait_recv()

        def one(sp, carry):
            for at in range(0, width, span):
                cols = slice(at, at + span)
                wg_ref[:, cols] += mm(grads_ref[zz * n_s + sp], buf[zz, sp, :, cols], 1, 0)
            return carry

        lax.fori_loop(0, n_s, one, 0)

    def over(t, act):
        for there, zz in level(t):
            @pl.when(there)
            def _():
                act(zz)

    own = pltpu.make_async_copy(normed_ref, buf.at[z, s], own_sem)
    own.start()

    @pl.when(z < n_z - 1)
    def _():
        zcopy(True, z, normed_ref).start()

    @pl.when(z > 0)
    def _():
        zcopy(False, z, normed_ref).start()

    @pl.when(s == n_s - 1)
    def _():
        hand_on(True)

    ccopy(z, x, normed_ref).start()

    @pl.when((s >= n_s // 2) & (s < n_s - 1))
    def _():
        hand_on(False)

    for j in range(1, n_x):
        xcopy(z, j, normed_ref).start()
    wg_ref[...] = jnp.zeros_like(wg_ref)
    own.wait()

    for t in range(1, n_z):
        for up, (there, zz) in zip((True, False), level(t)):
            @pl.when(there)
            def _():
                block = buf.at[zz, s]
                zcopy(up, zz, block).wait_recv()

                @pl.when((z < n_z - 1) if up else (z > 0))
                def _():
                    zcopy(up, zz, block).start()

                ccopy(zz, x, block).start()
                for j in range(1, n_x):
                    xcopy(zz, j, block).start()
        if t == 1:
            @pl.when(s < n_s // 2)
            def _():
                hand_on(False)
        over(t - 1, spread)
        if t > 1:
            over(t - 2, add)
    def heads_at(i, carry):
        doc, carried, rev = doc_ref[...], carried_ref[...], rev_ref[...]
        for h in range(blocks):
            cols = pl.ds(pl.multiple_of((i * blocks + h) * HS, HS), HS)
            backward_head(cols, doc, carried, rev, (q_ref, k_ref, v_ref, d_ref, st_ref, rst_ref),
                          dq_ref, dk_ref, dv_ref)
        return carry

    blocks = 4 if width % (4 * HS) == 0 else 1
    lax.fori_loop(0, width // (blocks * HS), heads_at, 0)
    over(n_z - 1, spread)
    for t in range(max(n_z - 2, 0), n_z):
        over(t, add)

    def drain(zz):
        for xs in range(n_x):
            ccopy(zz, xs, normed_ref).wait_send()
        for j in range(1, n_x):
            xcopy(zz, j, normed_ref).wait_send()

    for t in range(n_z):
        over(t, drain)
        for up, (there, zz) in zip((True, False), level(t) if t else ((z >= 0, z),) * 2):
            @pl.when(there & ((z < n_z - 1) if up else (z > 0)))
            def _():
                zcopy(up, zz, normed_ref).wait_send()

    @pl.when(s > 0)
    def _():
        kcopy().wait_send()


def gather_grad(grads, normed, local_r, joined, others, n_z, n_s):
    rows, width = normed.shape
    n_x = n_s // 2
    dma = pltpu.SemaphoreType.DMA
    vmem = pl.BlockSpec(memory_space=pltpu.VMEM)
    return pl.pallas_call(
        functools.partial(gather_body, n_z, n_s),
        out_shape=(
            jax.ShapeDtypeStruct((grads.shape[1], width), F32),
            *[jax.ShapeDtypeStruct((rows, width), BF16)] * 3,
        ),
        in_specs=[vmem] * (4 + len(others)),
        out_specs=[vmem] * 4,
        scratch_shapes=[
            pltpu.VMEM((HS, width), BF16),
            pltpu.VMEM((n_z, n_s, rows, width), BF16),
            pltpu.VMEM((HS, width), BF16),
            pltpu.VMEM((HS, width), BF16),
            dma((2, n_z)), dma((n_z,)),
            dma((n_z, n_x)), dma((n_z, n_x)),
            dma((n_z, n_x)), dma((n_z, n_x)),
            dma, dma, dma,
        ],
        compiler_params=pltpu.CompilerParams(collective_id=0, has_side_effects=True),
    )(grads, normed, local_r, joined, *others)


def neighbour(value, axis, step):
    peers, place = lax.axis_size(axis), lax.axis_index(axis)
    pairs = [(i, i + step) for i in range(peers) if 0 <= i + step < peers]
    got = lax.ppermute(jnp.broadcast_to(value, (1, HS)), axis, pairs)[0, 0]
    return jnp.where(place == (0 if step == 1 else peers - 1), -1.0, got)


def chain(local, joined, axis):
    got = jnp.zeros(local.shape, BF16)
    for hop in range(lax.axis_size(axis) - 1):
        sent = local if hop == 0 else local + jnp.where(joined, got.astype(F32), 0.0)
        got = got + lax.ppermute(sent.astype(BF16), axis, [(hop, hop + 1)])
    return got


def local(queries, key_rows, value_rows, row_plan, segments, norm_gain, out_weight, out_grad):
    row_total = queries.shape[0]
    width = queries.shape[1]
    heads = width // HS
    groups = lax.axis_size("dp")
    my_group = lax.axis_index("dp")
    devices = groups * lax.axis_size("seq")
    capacity = row_total // min(groups, 8) + row_total // 16
    groups_at = jnp.arange(groups, dtype=jnp.int32)
    below = (groups_at[:, None] < groups_at[None, :]).astype(jnp.int32)
    mine = (groups_at == my_group).astype(jnp.int32)
    to_others = jnp.sum(row_plan * mine[:, None], axis=0)
    to_me = jnp.sum(row_plan * mine[None, :], axis=1)
    my_send = jnp.sum(to_others[:, None] * below, axis=0)
    my_start = jnp.sum(to_me[:, None] * below, axis=0)
    slots = jnp.arange(capacity, dtype=jnp.int32)
    positions = jnp.arange(row_total, dtype=jnp.int32)
    send_index = jnp.minimum(my_send[:, None] + slots[None, :], row_total - 1)
    send_hot = (send_index[:, :, None] == positions[None, None, :]).astype(BF16)
    placed = positions[None, :, None] - my_start[:, None, None] == slots[None, None, :]
    pick_hot = (placed & (slots[None, None, :] < to_me[:, None, None])).astype(BF16)

    seg_f = segments[0].astype(F32)
    causal = positions[None, :] <= positions[:, None]
    same_doc = (causal & (seg_f[:, None] == seg_f[None, :])).astype(F32)
    tail = (seg_f == seg_f[-1]).astype(BF16)[:, None]
    head_part = (seg_f == seg_f[0]).astype(BF16)[:, None]

    q, k, v, local_state, d_normed, full_grad = exchange(
        send_hot, pick_hot, tail, queries, key_rows, value_rows, out_grad, out_weight,
        groups, lax.axis_size("mp"),
    )
    grad_cols = full_grad.transpose(0, 2, 1).reshape(devices, -1, row_total)
    grad_cols = lax.all_to_all(grad_cols, ("dp", "seq"), split_axis=0, concat_axis=0, tiled=True)

    half = jax.ShapeDtypeStruct((row_total, width), BF16)
    state = jax.ShapeDtypeStruct((HS, width), F32)
    edges, local_state = lax.optimization_barrier((seg_f, local_state))
    id_in = neighbour(edges[-1], "seq", 1)
    rid_in = neighbour(edges[0], "seq", -1)
    state_in = chain(local_state, id_in == seg_f[-1], "seq")
    carried = (seg_f == id_in).astype(F32)[:, None]
    gain_row = norm_gain.reshape(1, width)
    normed, d_half, local_r = by_heads(
        forward_body,
        heads,
        (same_doc, carried, head_part),
        (gain_row, q, k, v, state_in, d_normed),
        (half, half, state),
    )
    rejoined = jnp.broadcast_to((rid_in == seg_f[0]).astype(F32), (8, HS))
    rev_use = (seg_f == rid_in).astype(F32)[:, None]
    others = (same_doc, carried, rev_use, q, k, v, d_half, state_in)
    weight_grad, dquery, dkey, dvalue = gather_grad(
        grad_cols, normed, local_r, rejoined, others, groups, lax.axis_size("seq")
    )
    return normed, dquery, dkey, dvalue, weight_grad


def solution(mesh):
    placed = (
        P(("dp", "seq"), "mp"),
        P(("dp", "seq"), "mp"),
        P(("dp", "seq"), "mp"),
        P(),
        P("dp", "seq"),
        P("mp"),
        P("mp", None),
        P(("dp", "seq"), "mp"),
    )
    return jax.shard_map(
        local,
        mesh=mesh,
        in_specs=placed,
        out_specs=(
            P(("dp", "seq"), "mp"),
            P(("dp", "seq"), "mp"),
            P(("dp", "seq"), "mp"),
            P(("dp", "seq"), "mp"),
            P(("dp", "seq"), "mp"),
        ),
        check_vma=False,
    )
```
